512 devices in a mesh: dp: 8 (over x, core), expert: 64 (over y, z).
Axes of the slice: x: 4, y: 4, z: 16, core: 2. Of those that a mesh axis runs over, the one named last changes fastest.
Arguments:
- head_outputs: bfloat16 [65536, 8, 128], P(('dp', 'expert')), may hold values from -6 to 6
- out_grad: bfloat16 [65536, 4096], P(('dp', 'expert')), may hold values from -0.29882812 to 0.29882812
- gate_weights: bfloat16 [65536, 8], P(('dp', 'expert')), may hold values from 0.099609375 to 1
- route_ids: int32 [65536, 8], P(('dp', 'expert')), may hold values from 0 to 63, all different within a row; in each aligned block of 128 rows (0 to 127, 128 to 255, ...) at most 18 rows name the same one
- out_proj: bfloat16 [64, 128, 4096], P('expert'), may hold values from -0.5 to 0.5
Outputs:
- grad_head: bfloat16 [65536, 8, 128], P(('dp', 'expert'))
- grad_gate: bfloat16 [65536, 8], P(('dp', 'expert'))
- grad_proj: float32 [64, 128, 4096], P('expert', 'dp')
The draws below stay inside these ranges and needn't reach their ends.
Inputs may be any that keep to these rules, and one draw needn't show every extreme that they name: `route_ids`: each row names 8 different head experts. Within the 128 rows of one device no head expert is named by more than 18 rows, and in some devices' rows one is named by exactly 18.
All inputs are finite; a program needn't handle non-finite values.
Results may differ from the reference program's by a relative error of at most 0.0049.
Values may be sent and summed in bfloat16 or wider, within the bound.
A program may use at most 128 MiB of HBM per device.

```python
import math
import jax
import jax.numpy as jnp
import numpy as np
from jax import lax

D = 4096
HD = 128
TOPK = 8
T_DEV = 128
EXPERTS = 64
TOKENS = 65536
CAP = 18
DEVICES = 512


def steps_of(own_key, dims, shards, smallest, largest):
    factor_of, own = 1.0, jax.random.fold_in(own_key, 6)
    for dim, parts in shards:
        draws = jnp.exp(jax.random.uniform(jax.random.fold_in(own, dim), (parts,), jnp.float32, smallest / len(shards), largest / len(shards)))
        factor_of = factor_of * jnp.repeat(draws, dims[dim] // parts).reshape([-1 if axis == dim else 1 for axis in range(len(dims))])
    return factor_of


def deal_out(own_key, own, number, rows, amount, top, limit, slope):
    ranking = jax.random.permutation(own_key, amount)
    packed, common = portions_of(amount, rows * top, limit, slope, True), portions_of(amount, rows * top, limit, slope, False)
    places = jnp.arange(amount)

    def named(lengths, rotation):
        used = int((lengths > 0).sum())
        fixed = max(1, used // 4)
        shifted = fixed + (places - fixed + rotation * (used - fixed)) % max(1, amount - fixed)
        return jnp.zeros((amount,), jnp.int32).at[ranking[jnp.where(places < fixed, places, shifted)]].set(jnp.asarray(lengths, jnp.int32))

    lengths = jnp.where(number % 4 == 0, named(packed, number // 4), named(common, number - number // 4 - 1))
    mixed = jax.random.permutation(jax.random.fold_in(own, 3), amount)
    source_of, sink = mixed[0:amount // 2 * 2:2], mixed[1:amount // 2 * 2:2]
    margin = jnp.minimum(lengths[source_of] - 1, limit - lengths[sink]) // 2
    margin = jnp.where((source_of == ranking[0]) | (sink == ranking[0]) | (lengths[sink] == 0), 0, jnp.maximum(margin, 0))
    shifted = jax.random.randint(jax.random.fold_in(own, 4), (amount // 2,), 0, 1 << 20) % (margin + 1)
    lengths = lengths.at[source_of].add(-shifted).at[sink].add(shifted)
    members = jnp.searchsorted(jnp.cumsum(lengths), jnp.arange(rows * top), side="right").astype(jnp.int32)
    table = members.reshape(top, rows).T
    table = table[jax.random.permutation(jax.random.fold_in(own, 1), rows)]
    rotation = jax.random.randint(jax.random.fold_in(own, 2), (rows, 1), 0, top)
    return jnp.take_along_axis(table, (jnp.arange(top)[None, :] + rotation) % top, axis=1)


def portions_of(count, total, bound, skew, full):
    portions = [(1 << 20) // math.isqrt(rank ** skew) + 1 for rank in range(1, count + 1)]
    largest = bound if full else min(bound, max(-(-total // count), total * portions[0] // sum(portions)))
    least = 1 if total - largest >= count - 1 else 0
    holding, rest = [largest] + [least] * (count - 1), total - largest - least * (count - 1)
    while rest > 0:
        free = [i for i in range(1, count) if holding[i] < largest] or [i for i in range(1, count) if holding[i] < bound]
        whole, left = sum([portions[i] for i in free]), rest
        for i in free:
            extra = min(bound - holding[i], max(1, left * portions[i] // whole), rest)
            holding[i] = holding[i] + extra
            rest = rest - extra
    return np.array(holding)


def noise(key, extent, deviation, bound, cuts=(), kind=jnp.bfloat16):
    entries = deviation * jax.random.normal(key, extent, jnp.float32)
    if cuts:
        entries = entries * steps_of(key, extent, cuts, -0.22, 0.18)
    return jnp.clip(entries, -bound, bound).astype(kind)


def setup_inputs(seed: int = 0) -> dict:
    keys = jax.random.split(jax.random.key(seed), 6)
    head_outputs = noise(keys[0], (TOKENS, TOPK, HD), 1.0, 6.0, ((0, 512),))
    out_grad = noise(keys[1], (TOKENS, D), 0.05, 0.29882812, ((0, 512),))
    gate_weights = jnp.clip(0.099609375 + 0.9003906 * jax.random.uniform(keys[2], (TOKENS, TOPK), jnp.float32) ** steps_of(keys[2], (TOKENS, TOPK), ((0, 512),), -0.2, 0.2), 0.099609375, 1.0).astype(jnp.bfloat16)
    route_ids_keys = jax.random.split(jax.random.fold_in(keys[3], 1), TOKENS // T_DEV)
    route_ids_turns = jax.random.permutation(jax.random.fold_in(keys[3], 3), TOKENS // T_DEV)
    route_ids = jax.vmap(lambda own, number: deal_out(jax.random.fold_in(keys[3], 2), own, number, T_DEV, EXPERTS, TOPK, CAP, 2))(route_ids_keys, route_ids_turns).reshape((TOKENS, TOPK))
    out_proj = noise(keys[4], (EXPERTS, HD, D), HD ** -0.5, 0.5, ((0, 64),))
    return dict(head_outputs=head_outputs, out_grad=out_grad, gate_weights=gate_weights, route_ids=route_ids, out_proj=out_proj)


soft_cap = 1.5


def reference(head_outputs, out_grad, gate_weights, route_ids, out_proj):
    pair_count = TOKENS * TOPK
    local_pairs = T_DEV * TOPK
    slot_total = DEVICES * CAP
    flat_routes = route_ids.reshape(pair_count)
    one_hot = (flat_routes[:, None] == jnp.arange(EXPERTS, dtype=jnp.int32)[None, :]).astype(jnp.int32)
    one_hot = one_hot.reshape(DEVICES, local_pairs, EXPERTS)
    before = jnp.cumsum(one_hot, axis=1) - one_hot
    position = jnp.sum(before * one_hot, axis=2).reshape(pair_count).astype(jnp.int32)
    device_of = (jnp.arange(pair_count, dtype=jnp.int32) // local_pairs).astype(jnp.int32)
    target = (flat_routes * slot_total + device_of * CAP + position).astype(jnp.int32)
    slot_table = jnp.full((EXPERTS * slot_total,), pair_count, jnp.int32)
    slot_table = slot_table.at[target].set(jnp.arange(pair_count, dtype=jnp.int32)).reshape(EXPERTS, slot_total)
    heads_flat = head_outputs.reshape(pair_count, HD)
    gates_flat = gate_weights.reshape(pair_count)

    def one_expert(expert_item):
        slot_index, weight = expert_item
        grad_rows = jnp.take(out_grad, slot_index // TOPK, axis=0, mode="fill", fill_value=0)
        head_rows = jnp.take(heads_flat, slot_index, axis=0, mode="fill", fill_value=0)
        gate_rows = jnp.take(gates_flat, slot_index, axis=0, mode="fill", fill_value=0)
        pre_cap = jnp.dot(head_rows, weight, preferred_element_type=jnp.float32)
        capped = jnp.tanh(pre_cap / soft_cap)
        grad_pre = (gate_rows[:, None].astype(jnp.float32) * grad_rows.astype(jnp.float32) * (1.0 - capped * capped)).astype(jnp.bfloat16)
        head_grad = jnp.dot(grad_pre, weight.T, preferred_element_type=jnp.float32).astype(jnp.bfloat16)
        gate_grad = jnp.sum(grad_rows.astype(jnp.float32) * (soft_cap * capped), axis=1).astype(jnp.bfloat16)
        weight_grad = jnp.dot(head_rows.T, grad_pre, preferred_element_type=jnp.float32)
        return head_grad, gate_grad, weight_grad

    head_grads, gate_grads, grad_proj = lax.map(one_expert, (slot_table, out_proj))
    flat_table = slot_table.reshape(EXPERTS * slot_total)
    grad_head = jnp.zeros((pair_count, HD), jnp.bfloat16).at[flat_table].set(head_grads.reshape(EXPERTS * slot_total, HD), mode="drop")
    grad_gate = jnp.zeros((pair_count,), jnp.bfloat16).at[flat_table].set(gate_grads.reshape(EXPERTS * slot_total), mode="drop")
    return grad_head.reshape(TOKENS, TOPK, HD), grad_gate.reshape(TOKENS, TOPK), grad_proj
```

```python
import functools

import jax
import jax.numpy as jnp
from jax import lax
from jax.experimental import pallas as pl
from jax.experimental.pallas import tpu as pltpu
from jax.sharding import PartitionSpec as P

CAP = 1.5
F32 = jnp.float32
BF16 = jnp.bfloat16

SRC = 8
OWN = 8
TOK = 128
TOPK = 8
HD = 128
D = 4096
MAIN = 16
OVER = 2
ROWS = SRC * (MAIN + OVER)
META = D + TOPK * HD
WIDE = META + 128
STEP = 512


def iota(shape, axis):
    return lax.broadcasted_iota(jnp.int32, shape, axis).astype(F32)


def dispatch(base, x_ref, gx, gh, gg, hcat, qm, qo, po, over):
    upper = (iota((TOK, TOK), 0) < iota((TOK, TOK), 1)).astype(BF16)
    lane = iota((TOK, 128), 1)
    slot = iota((MAIN, TOK), 0)
    over[...] = jnp.zeros_like(over)

    def one_source(s, _):
        meta = x_ref[s, :, META:WIDE].astype(F32)
        routes = meta.T[TOPK : 2 * TOPK, :]
        named = [(routes == (base + 2 * j).astype(F32)).astype(F32) for j in range(OWN)]
        chosen = jnp.concatenate([jnp.sum(n, axis=0, keepdims=True) for n in named], axis=0)
        before = jnp.dot(chosen.astype(BF16), upper, preferred_element_type=F32)
        shift = (OVER * s - MAIN).astype(F32)
        columns = pl.ds(pl.multiple_of(s * TOK, TOK), TOK)
        picks = []
        for j in range(OWN):
            rows = slice(j * MAIN, (j + 1) * MAIN)
            pos = before[j : j + 1, :]
            spot = jnp.where(chosen[j : j + 1, :] > 0, pos, -1.0)
            picks.append((spot == slot).astype(F32))
            late = jnp.where(spot >= MAIN, spot + shift, -1.0)
            po[rows, columns] = (late == slot).astype(F32).astype(BF16)
            own = jnp.where(named[j] > 0, pos, -1.0)
            own_late = jnp.where(own >= MAIN, own + shift, -1.0)
            for k in range(TOPK):
                part = slice(k * TOK, (k + 1) * TOK)
                qm[rows, part] = (own[k : k + 1, :] == slot).astype(F32).astype(BF16)
                qo[rows, part] = (own_late[k : k + 1, :] == slot).astype(F32).astype(BF16)
        pick = jnp.concatenate(picks, axis=0).astype(BF16)
        for k in range(TOPK):
            part = slice(k * TOK, (k + 1) * TOK)
            hcat[part, 0:HD] = x_ref[s, :, D + k * HD : D + (k + 1) * HD]
            hcat[part, HD : 2 * HD] = jnp.where(lane == k, meta, 0.0).astype(BF16)
        out_rows = pl.ds(pl.multiple_of(s * MAIN, MAIN), MAIN)
        for c in range(0, D, STEP):
            block = jnp.dot(pick, x_ref[s, :, c : c + STEP], preferred_element_type=F32)
            gx[:, out_rows, c : c + STEP] = block.astype(BF16).reshape(OWN, MAIN, STEP)
        block = jnp.dot(qm[...], hcat[...], preferred_element_type=F32)
        gh[:, out_rows, :] = block[:, 0:HD].astype(BF16).reshape(OWN, MAIN, HD)
        gate = jnp.sum(block[:, HD:], axis=1, keepdims=True)
        gg[:, out_rows, :] = jnp.broadcast_to(gate, (OWN * MAIN, 128)).reshape(OWN, MAIN, 128)
        over[...] += jnp.dot(qo[...], hcat[...], preferred_element_type=F32)
        return 0

    lax.fori_loop(0, SRC, one_source, 0)
    tail = slice(SRC * MAIN, ROWS)
    width = 2 * 128
    for c in range(0, D, width):
        tokens = x_ref[:, :, c : c + width].reshape(SRC * TOK, width)
        block = jnp.dot(po[...], tokens, preferred_element_type=F32)
        gx[:, tail, c : c + width] = block.astype(BF16).reshape(OWN, SRC * OVER, width)
    gh[:, tail, :] = over[:, 0:HD].astype(BF16).reshape(OWN, SRC * OVER, HD)
    gate = jnp.sum(over[:, HD:], axis=1, keepdims=True)
    gg[:, tail, :] = jnp.broadcast_to(gate, (OWN * SRC * OVER, 128)).reshape(OWN, SRC * OVER, 128)


def owner_kernel(x_ref, w_ref, dw_ref, back_ref, gx, gh, gg, hcat, qm, qo, po, over):
    j = pl.program_id(0)
    me = lax.axis_index("dp")

    @pl.when(j == 0)
    def _():
        base = (me // 2) * 16 + lax.rem(me, 2)
        dispatch(base, x_ref, gx, gh, gg, hcat, qm, qo, po, over)

    heads = gh[j]
    gate = gg[j]
    head_grad = jnp.zeros((ROWS, HD), F32)
    gate_sum = jnp.zeros((ROWS, 128), F32)
    for c in range(0, D, STEP):
        weight = w_ref[:, 0, :, :, c : c + STEP].reshape(HD, STEP)
        pre = jnp.dot(heads, weight, preferred_element_type=F32)
        capped = jnp.tanh(pre * (1.0 / CAP))
        grad = gx[j, :, c : c + STEP].astype(F32)
        grad_capped = grad * capped
        rest = grad - grad_capped * capped
        parts = []
        for b in range(0, STEP, 128):
            gate_sum = gate_sum + grad_capped[:, b : b + 128]
            parts.append((gate * rest[:, b : b + 128]).astype(BF16))
        grad_pre = jnp.concatenate(parts, axis=1)
        head_grad = head_grad + lax.dot_general(
            grad_pre, weight, (((1,), (1,)), ((), ())), preferred_element_type=F32
        )
        grown = lax.dot_general(
            heads, grad_pre, (((0,), (0,)), ((), ())), preferred_element_type=F32
        )
        dw_ref[:, 0, :, :, c : c + STEP] = grown.astype(dw_ref.dtype).reshape(4, 2, 16, STEP)
    gate_grad = CAP * jnp.sum(gate_sum, axis=1, keepdims=True)
    back_ref[0, :, 0:HD] = head_grad.astype(BF16)
    back_ref[0, :, HD : 2 * HD] = jnp.broadcast_to(gate_grad, (ROWS, 128)).astype(BF16)


def owner_work(tokens, weights, sum_type):
    full = (4, 1, 2, 16, D)
    at_expert = lambda j: (0, j, 0, 0, 0)
    return pl.pallas_call(
        owner_kernel,
        grid=(OWN,),
        out_shape=(
            jax.ShapeDtypeStruct((4, OWN, 2, 16, D), sum_type),
            jax.ShapeDtypeStruct((OWN, ROWS, 2 * HD), BF16),
        ),
        in_specs=[
            pl.BlockSpec((SRC, TOK, WIDE), lambda j: (0, 0, 0), pipeline_mode=pl.Buffered(1)),
            pl.BlockSpec(full, at_expert),
        ],
        out_specs=(
            pl.BlockSpec(full, at_expert),
            pl.BlockSpec((1, ROWS, 2 * HD), lambda j: (j, 0, 0)),
        ),
        scratch_shapes=[
            pltpu.VMEM((OWN, ROWS, D), BF16),
            pltpu.VMEM((OWN, ROWS, HD), BF16),
            pltpu.VMEM((OWN, ROWS, 128), F32),
            pltpu.VMEM((TOPK * TOK, 2 * HD), BF16),
            pltpu.VMEM((OWN * MAIN, TOPK * TOK), BF16),
            pltpu.VMEM((OWN * MAIN, TOPK * TOK), BF16),
            pltpu.VMEM((OWN * MAIN, SRC * TOK), BF16),
            pltpu.VMEM((OWN * MAIN, 2 * HD), F32),
        ],
        compiler_params=pltpu.CompilerParams(vmem_limit_bytes=60 << 20),
    )(tokens, weights)


def return_kernel(routes_ref, back_ref, head_ref, gate_ref):
    routes = routes_ref[...]
    experts = lax.broadcasted_iota(jnp.int32, (TOK, 128), 1)
    named = [(routes[:, k : k + 1] == experts).astype(F32) for k in range(TOPK)]
    chosen = functools.reduce(lambda a, b: a + b, named)
    lower = (iota((TOK, TOK), 1) < iota((TOK, TOK), 0)).astype(BF16)
    before = jnp.dot(lower, chosen.astype(BF16), preferred_element_type=F32)
    rows = lax.broadcasted_iota(jnp.int32, (TOK, SRC * ROWS), 1)
    gates = jnp.zeros((TOK, 128), F32)
    for k in range(TOPK):
        expert = routes[:, k : k + 1]
        slot = jnp.sum(named[k] * before, axis=1, keepdims=True).astype(jnp.int32)
        owner = 2 * (expert >> 4) + (expert & 1)
        index = (expert & 15) >> 1
        place = jnp.where(
            slot < MAIN, index * MAIN + slot, OWN * MAIN + OVER * index + slot - MAIN
        )
        pick = (rows == owner * ROWS + place).astype(F32).astype(BF16)
        block = jnp.dot(pick, back_ref[...], preferred_element_type=F32)
        head_ref[:, k * HD : (k + 1) * HD] = block[:, 0:HD].astype(BF16)
        gates = jnp.where(experts == k, block[:, HD:], gates)
    gate_ref[...] = gates[:, 0:TOPK].astype(BF16)


def put_back(routes, back):
    return pl.pallas_call(
        return_kernel,
        out_shape=(
            jax.ShapeDtypeStruct((TOK, TOPK * HD), BF16),
            jax.ShapeDtypeStruct((TOK, TOPK), BF16),
        ),
        compiler_params=pltpu.CompilerParams(vmem_limit_bytes=32 << 20),
    )(routes, back)


def swap_pairs(mesh):
    pairs = []
    for dp in range(mesh.shape["dp"]):
        for expert in range(mesh.shape["expert"]):
            x, core = divmod(dp, 2)
            y, z = divmod(expert, 16)
            to_dp = 2 * y + z % 2
            to_expert = 16 * x + z - z % 2 + core
            pairs.append((dp * 64 + expert, to_dp * 64 + to_expert))
    return pairs


def local(head_outputs, out_grad, gate_weights, route_ids, out_proj, pairs, sum_type=F32):
    axes = ("dp", "expert")
    me = lax.axis_index("dp")
    part = lax.dynamic_slice_in_dim(out_proj[0], me * 16, 16, 0)
    part = lax.ppermute(part, axes, pairs)
    weights = lax.all_gather(part, "expert")
    packed = jnp.concatenate(
        [
            out_grad,
            head_outputs.reshape(TOK, TOPK * HD),
            gate_weights,
            route_ids.astype(BF16),
            jnp.zeros((TOK, 128 - 2 * TOPK), BF16),
        ],
        axis=1,
    )
    tokens = lax.all_gather(packed, "dp")
    sums, back = owner_work(tokens, weights.reshape(4, OWN, 2, 16, D), sum_type)
    grad_proj = lax.psum_scatter(
        sums.reshape(64, 16, D), "expert", scatter_dimension=0, tiled=False
    )
    grad_proj = lax.ppermute(grad_proj.astype(F32), axes, pairs)
    main = back[:, : SRC * MAIN].reshape(OWN, SRC, MAIN, 2 * HD).transpose(1, 0, 2, 3)
    late = back[:, SRC * MAIN :].reshape(OWN, SRC, OVER, 2 * HD).transpose(1, 0, 2, 3)
    send = jnp.concatenate(
        [main.reshape(SRC, OWN * MAIN, 2 * HD), late.reshape(SRC, OWN * OVER, 2 * HD)], axis=1
    )
    got = lax.all_to_all(send, "dp", split_axis=0, concat_axis=0, tiled=True)
    grad_head, grad_gate = put_back(route_ids, got.reshape(SRC * ROWS, 2 * HD))
    return grad_head.reshape(TOK, TOPK, HD), grad_gate, grad_proj[None]


def solution(mesh):
    return jax.shard_map(
        functools.partial(local, pairs=swap_pairs(mesh)),
        mesh=mesh,
        in_specs=(
            P(("dp", "expert"), None, None),
            P(("dp", "expert"), None),
            P(("dp", "expert"), None),
            P(("dp", "expert"), None),
            P("expert", None, None),
        ),
        out_specs=(
            P(("dp", "expert"), None, None),
            P(("dp", "expert"), None),
            P("expert", "dp", None),
        ),
        check_vma=False,
    )
```

```python
import functools

import jax
import jax.numpy as jnp
from jax import lax
from jax.experimental import pallas as pl
from jax.experimental.pallas import tpu as pltpu
from jax.sharding import PartitionSpec as P

CAP = 1.5
F32 = jnp.float32
BF16 = jnp.bfloat16

SRC = 8
OWN = 8
TOK = 128
TOPK = 8
HD = 128
D = 4096
MAIN = 16
OVER = 2
ROWS = SRC * (MAIN + OVER)
META = D + TOPK * HD
WIDE = META + 128
STEP = 512


def iota(shape, axis):
    return lax.broadcasted_iota(jnp.int32, shape, axis).astype(F32)


def dispatch(base, x_ref, gx, gh, gg, hcat, qm, qo, po, over, arrived):
    upper = (iota((TOK, TOK), 0) < iota((TOK, TOK), 1)).astype(BF16)
    lane = iota((TOK, 128), 1)
    slot = iota((MAIN, TOK), 0)
    over[...] = jnp.zeros_like(over)

    def one_source(s, _):
        arrived(s)
        meta = x_ref[s, :, META:WIDE].astype(F32)
        routes = meta.T[TOPK : 2 * TOPK, :]
        named = [(routes == (base + 2 * j).astype(F32)).astype(F32) for j in range(OWN)]
        chosen = jnp.concatenate([jnp.sum(n, axis=0, keepdims=True) for n in named], axis=0)
        before = jnp.dot(chosen.astype(BF16), upper, preferred_element_type=F32)
        shift = (OVER * s - MAIN).astype(F32)
        columns = pl.ds(pl.multiple_of(s * TOK, TOK), TOK)
        picks = []
        for j in range(OWN):
            rows = slice(j * MAIN, (j + 1) * MAIN)
            pos = before[j : j + 1, :]
            spot = jnp.where(chosen[j : j + 1, :] > 0, pos, -1.0)
            picks.append((spot == slot).astype(F32))
            late = jnp.where(spot >= MAIN, spot + shift, -1.0)
            po[rows, columns] = (late == slot).astype(F32).astype(BF16)
            own = jnp.where(named[j] > 0, pos, -1.0)
            own_late = jnp.where(own >= MAIN, own + shift, -1.0)
            for k in range(TOPK):
                part = slice(k * TOK, (k + 1) * TOK)
                qm[rows, part] = (own[k : k + 1, :] == slot).astype(F32).astype(BF16)
                qo[rows, part] = (own_late[k : k + 1, :] == slot).astype(F32).astype(BF16)
        pick = jnp.concatenate(picks, axis=0).astype(BF16)
        for k in range(TOPK):
            part = slice(k * TOK, (k + 1) * TOK)
            hcat[part, 0:HD] = x_ref[s, :, D + k * HD : D + (k + 1) * HD]
            hcat[part, HD : 2 * HD] = jnp.where(lane == k, meta, 0.0).astype(BF16)
        out_rows = pl.ds(pl.multiple_of(s * MAIN, MAIN), MAIN)
        for c in range(0, D, STEP):
            block = jnp.dot(pick, x_ref[s, :, c : c + STEP], preferred_element_type=F32)
            gx[:, out_rows, c : c + STEP] = block.astype(BF16).reshape(OWN, MAIN, STEP)
        block = jnp.dot(qm[...], hcat[...], preferred_element_type=F32)
        gh[:, out_rows, :] = block[:, 0:HD].astype(BF16).reshape(OWN, MAIN, HD)
        gate = jnp.sum(block[:, HD:], axis=1, keepdims=True)
        gg[:, out_rows, :] = jnp.broadcast_to(gate, (OWN * MAIN, 128)).reshape(OWN, MAIN, 128)
        over[...] += jnp.dot(qo[...], hcat[...], preferred_element_type=F32)
        return 0

    lax.fori_loop(0, SRC, one_source, 0)
    tail = slice(SRC * MAIN, ROWS)
    width = 2 * 128
    for c in range(0, D, width):
        tokens = x_ref[:, :, c : c + width].reshape(SRC * TOK, width)
        block = jnp.dot(po[...], tokens, preferred_element_type=F32)
        gx[:, tail, c : c + width] = block.astype(BF16).reshape(OWN, SRC * OVER, width)
    gh[:, tail, :] = over[:, 0:HD].astype(BF16).reshape(OWN, SRC * OVER, HD)
    gate = jnp.sum(over[:, HD:], axis=1, keepdims=True)
    gg[:, tail, :] = jnp.broadcast_to(gate, (OWN * SRC * OVER, 128)).reshape(OWN, SRC * OVER, 128)


MESH = pl.DeviceIdType.MESH
HALF = D // 2
FAR = 8


def place():
    dp, expert = lax.axis_index("dp"), lax.axis_index("expert")
    y, z = expert // 16, lax.rem(expert, 16)
    x, core = dp // 2, lax.rem(dp, 2)
    odd = lax.rem(z, 2)
    partner = (2 * y + odd, 16 * x + z - odd + core)
    alone = jnp.logical_and(x == y, core == odd)
    return dp, y, z, partner, alone


def meet(peers, partner, alone):
    barrier = pltpu.get_barrier_semaphore()
    for peer in peers:
        pl.semaphore_signal(barrier, inc=1, device_id=peer, device_id_type=MESH)

    @pl.when(jnp.logical_not(alone))
    def _():
        pl.semaphore_signal(barrier, inc=1, device_id=partner, device_id_type=MESH)

    pl.semaphore_wait(barrier, len(peers) + jnp.where(alone, 0, 1))


def send(src, dst, send_sem, recv_sem, device):
    return pltpu.make_async_remote_copy(
        src_ref=src,
        dst_ref=dst,
        send_sem=send_sem,
        recv_sem=recv_sem,
        device_id=device,
        device_id_type=MESH,
    )


def gather_kernel(proj_ref, w_ref, own, own_sem, keep_sem, zs, zr, ys, yr, fs, fr):
    dp, y, z, partner, alone = place()
    at = lambda row, col: (dp, row * 16 + col)
    ring = lambda v, step, n: lax.rem(v + step + n, n)
    up, down = at(ring(y, 1, 4), z), at(ring(y, -1, 4), z)
    right, left = at(y, ring(z, 1, 16)), at(y, ring(z, -1, 16))
    meet((up, down, right, left), partner, alone)

    mine = proj_ref.at[pl.ds(pl.multiple_of(dp * 16, 16), 16), :]
    trade = send(mine, own, own_sem.at[0], own_sem.at[1], partner)
    local = pltpu.make_async_copy(mine, own, own_sem.at[1])

    @pl.when(alone)
    def _():
        local.start()
        local.wait()

    @pl.when(jnp.logical_not(alone))
    def _():
        trade.start()
        trade.wait()

    keep = pltpu.make_async_copy(own, w_ref.at[y, z], keep_sem)
    keep.start()

    def along_z(src, col, way, hop):
        return send(src, w_ref.at[y, col], zs.at[way, hop], zr.at[way, hop], (right, left)[way])

    def along_y(src, col, way):
        return send(src, w_ref.at[y, col], ys.at[way, col], yr.at[way, col], (up, down)[way])

    def spread(src, col):
        along_y(src, col, 0).start()
        along_y(src, col, 1).start()

    along_z(own, z, 0, 0).start()
    along_z(own, z, 1, 0).start()
    spread(own, z)
    for hop in range(1, FAR + 1):
        for way in range(2 if hop < FAR else 1):
            col = ring(z, -hop if way == 0 else hop, 16)
            block = w_ref.at[y, col]
            along_z(block, col, way, hop - 1).wait_recv()
            if hop < FAR - way:
                along_z(block, col, way, hop).start()
            spread(block, col)

    def forward(row, col, way):
        half = pl.ds(way * HALF, HALF)
        block = w_ref.at[row, col, :, half]
        return send(block, block, fs.at[way, col], fr.at[way, col], (up, down)[way])

    below, above, across = ring(y, -1, 4), ring(y, 1, 4), ring(y, 2, 4)
    order = [0]
    for hop in range(1, FAR + 1):
        order += [-hop, hop] if hop < FAR else [-hop]
    for step in order:
        col = ring(z, step, 16)
        send(own, w_ref.at[below, col], ys.at[0, col], yr.at[0, col], up).wait_recv()
        forward(below, col, 0).start()
        send(own, w_ref.at[above, col], ys.at[1, col], yr.at[1, col], down).wait_recv()
        forward(above, col, 1).start()
    for step in order:
        col = ring(z, step, 16)
        forward(across, col, 0).wait_recv()
        forward(across, col, 1).wait_recv()
    keep.wait()
    for hop in range(FAR):
        for way in range(2):
            if hop < FAR - way:
                along_z(own, z, way, hop).wait_send()
    for col in range(16):
        for way in range(2):
            along_y(own, col, way).wait_send()
            forward(across, col, way).wait_send()


def gather_weights(proj):
    sems = pltpu.SemaphoreType.DMA
    return pl.pallas_call(
        gather_kernel,
        out_shape=jax.ShapeDtypeStruct((4, 16, 16, D), BF16),
        in_specs=[pl.BlockSpec(memory_space=pl.ANY)],
        out_specs=pl.BlockSpec(memory_space=pl.ANY),
        scratch_shapes=[
            pltpu.VMEM((16, D), BF16),
            sems((2,)),
            sems,
            sems((2, FAR)),
            sems((2, FAR)),
            sems((2, 16)),
            sems((2, 16)),
            sems((2, 16)),
            sems((2, 16)),
        ],
        compiler_params=pltpu.CompilerParams(collective_id=0, has_side_effects=True),
        cost_estimate=pl.CostEstimate(flops=0, bytes_accessed=1 << 28, transcendentals=0),
    )(proj)


def expert_step(i, j, wbuf, slot, gx, gh, gg, part, ret, late):
    heads = gh[j]
    gate = gg[j]
    head_grad = jnp.zeros((ROWS, HD), F32)
    gate_sum = jnp.zeros((ROWS, 128), F32)
    for c in range(0, D, STEP):
        weight = wbuf[slot, :, :, :, c : c + STEP].reshape(HD, STEP)
        pre = jnp.dot(heads, weight, preferred_element_type=F32)
        capped = jnp.tanh(pre * (1.0 / CAP))
        grad = gx[j, :, c : c + STEP].astype(F32)
        grad_capped = grad * capped
        rest = grad - grad_capped * capped
        parts = []
        for b in range(0, STEP, 128):
            gate_sum = gate_sum + grad_capped[:, b : b + 128]
            parts.append((gate * rest[:, b : b + 128]).astype(BF16))
        grad_pre = jnp.concatenate(parts, axis=1)
        head_grad = head_grad + lax.dot_general(
            grad_pre, weight, (((1,), (1,)), ((), ())), preferred_element_type=F32
        )
        grown = lax.dot_general(
            heads, grad_pre, (((0,), (0,)), ((), ())), preferred_element_type=F32
        )
        part[i, :, :, c : c + STEP] = grown.astype(BF16).reshape(4, 32, STEP)
    gate_grad = CAP * jnp.sum(gate_sum, axis=1, keepdims=True)
    both = jnp.concatenate([head_grad, jnp.broadcast_to(gate_grad, (ROWS, 128))], axis=1)
    both = both.astype(BF16)
    rows = pl.ds(pl.multiple_of(j * MAIN, MAIN), MAIN)
    ret[:, rows, :] = both[0 : SRC * MAIN].reshape(SRC, MAIN, 2 * HD)
    late[rows, :] = both[SRC * MAIN :]


def owner_kernel(
    x_ref, w_ref, out_ref, got_ref,
    xbuf, wbuf, gx, gh, gg, hcat, qm, qo, po, over, part, a_in, b_in, comb, zl, zr, zout, ret, late,
    x_sem, w_sem, ps, pr, cs, cr, zs, zlr, zrr, out_sem, rs, rr, keep_sem,
):
    dp, y, z, partner, alone = place()
    ring = lambda v, step, n: lax.rem(v + step + n, n)
    yu, yd, y2 = ring(y, 1, 4), ring(y, -1, 4), ring(y, 2, 4)
    up, down = (dp, yu * 16 + z), (dp, yd * 16 + z)
    right, left = (dp, y * 16 + ring(z, 1, 16)), (dp, y * 16 + ring(z, -1, 16))
    here = y * 16 + z
    others = [(lax.rem(dp + k, SRC), here) for k in range(1, SRC)]
    base = (dp // 2) * 16 + lax.rem(dp, 2)

    def expert_at(i):
        away = 4 - (i + 1) // 2
        return lax.rem(z // 2 + OWN + jnp.where(lax.rem(i, 2) == 1, away, -away), OWN)

    def token_copy(s):
        return pltpu.make_async_copy(x_ref.at[s], xbuf.at[s], x_sem.at[s])

    def weight_copy(i):
        slot = lax.rem(i, 2)
        return pltpu.make_async_copy(w_ref.at[:, expert_at(i)], wbuf.at[slot], w_sem.at[slot])

    for s in range(SRC):
        token_copy(s).start()
    weight_copy(0).start()
    meet([up, down, right, left] + others, partner, alone)
    dispatch(base, xbuf, gx, gh, gg, hcat, qm, qo, po, over, lambda s: token_copy(s).wait())

    low, high = pl.ds(0, HALF), pl.ds(HALF, HALF)

    def first_sends(i):
        return (
            send(part.at[i, y2, :, low], a_in.at[i, 0], ps.at[i, 0], pr.at[i, 0], up),
            send(part.at[i, y2, :, high], a_in.at[i, 1], ps.at[i, 1], pr.at[i, 1], down),
            send(part.at[i, yu, :, high], b_in.at[i, 0, :, high], ps.at[i, 2], pr.at[i, 2], up),
            send(part.at[i, yd, :, low], b_in.at[i, 1, :, low], ps.at[i, 3], pr.at[i, 3], down),
        )

    def second_sends(i):
        return (
            send(comb.at[i, 0], b_in.at[i, 0, :, low], cs.at[i, 0], cr.at[i, 0], up),
            send(comb.at[i, 1], b_in.at[i, 1, :, high], cs.at[i, 1], cr.at[i, 1], down),
        )

    def combine(i):
        first, second = first_sends(i), second_sends(i)
        first[0].wait_recv()
        comb[i, 0] = (part[i, yu, :, low].astype(F32) + a_in[i, 0].astype(F32)).astype(BF16)
        second[0].start()
        first[1].wait_recv()
        comb[i, 1] = (part[i, yd, :, high].astype(F32) + a_in[i, 1].astype(F32)).astype(BF16)
        second[1].start()

    def to_right(k, slot):
        return send(zout.at[k], zl.at[slot], zs.at[k], zlr.at[slot], right)

    def to_left(k, slot):
        return send(zout.at[k], zr.at[slot], zs.at[k], zrr.at[slot], left)

    def to_partner(k):
        return send(zout.at[k], out_ref, zs.at[k], out_sem, partner)

    def finish(i):
        for one in first_sends(i)[2:] + second_sends(i):
            one.wait_recv()
        total = (
            part[i, y].astype(F32) + b_in[i, 0].astype(F32) + b_in[i, 1].astype(F32)
        )
        j = expert_at(i)
        for c in range(2):
            k = 2 * i + c
            zout[k] = total[16 * c : 16 * (c + 1)]
            ahead = lax.rem(2 * j + c - z + 16, 16)
            behind = lax.rem(16 - ahead, 16)

            @pl.when(ahead < FAR)
            def _():
                to_right(k, ahead).wait_recv()
                zout[k] += zl[ahead]

            @pl.when(behind < FAR - 1)
            def _():
                to_left(k, behind).wait_recv()
                zout[k] += zr[behind]

            @pl.when(jnp.logical_and(ahead >= 1, ahead <= FAR))
            def _():
                to_right(k, ahead - 1).start()

            @pl.when(ahead > FAR)
            def _():
                to_left(k, behind - 1).start()

            @pl.when(jnp.logical_and(ahead == 0, alone))
            def _():
                pltpu.make_async_copy(zout.at[k], out_ref, zs.at[k]).start()

            @pl.when(jnp.logical_and(ahead == 0, jnp.logical_not(alone)))
            def _():
                to_partner(k).start()

    def returns():
        out = []
        for k in range(1, SRC):
            to = lax.rem(dp + k, SRC)
            out.append(send(ret.at[to], got_ref.at[dp], rs.at[k], rr.at[k], others[k - 1]))
        return out

    keep = pltpu.make_async_copy(ret.at[dp], got_ref.at[dp], keep_sem)

    def one_expert(i, _):
        @pl.when(i < OWN)
        def _():
            @pl.when(i + 1 < OWN)
            def _():
                weight_copy(i + 1).start()

            weight_copy(i).wait()
            expert_step(i, expert_at(i), wbuf, lax.rem(i, 2), gx, gh, gg, part, ret, late)
            for one in first_sends(i):
                one.start()

        @pl.when(i == OWN - 1)
        def _():
            to = lax.broadcasted_iota(jnp.int32, (OWN * MAIN, OWN * MAIN), 0)
            source = lax.broadcasted_iota(jnp.int32, (OWN * MAIN, OWN * MAIN), 1)
            want = (lax.rem(to, 16) // 2) * 16 + (to // 16) * 2 + lax.rem(to, 2)
            shuffle = (source == want).astype(F32).astype(BF16)
            moved = jnp.dot(shuffle, late[...], preferred_element_type=F32).astype(BF16)
            ret[:, OWN * MAIN :, :] = moved.reshape(SRC, OWN * OVER, 2 * HD)
            for one in returns():
                one.start()
            keep.start()

        @pl.when(jnp.logical_and(i >= 1, i <= OWN))
        def _():
            combine(i - 1)

        @pl.when(i >= 2)
        def _():
            finish(i - 2)

        return 0

    lax.fori_loop(0, OWN + 2, one_expert, 0)
    for one in returns():
        one.wait()
    keep.wait()

    @pl.when(jnp.logical_not(alone))
    def _():
        to_partner(0).wait_recv()

    def drain(i, _):
        for one in first_sends(i) + second_sends(i):
            one.wait_send()
        to_right(2 * i, 0).wait_send()
        to_right(2 * i + 1, 0).wait_send()
        return 0

    lax.fori_loop(0, OWN, drain, 0)


def owner_work(tokens, weights):
    sems = pltpu.SemaphoreType.DMA
    vmem = pltpu.VMEM
    return pl.pallas_call(
        owner_kernel,
        out_shape=(
            jax.ShapeDtypeStruct((16, D), F32),
            jax.ShapeDtypeStruct((SRC, ROWS, 2 * HD), BF16),
        ),
        in_specs=[pl.BlockSpec(memory_space=pl.ANY)] * 2,
        out_specs=(pl.BlockSpec(memory_space=pl.ANY),) * 2,
        scratch_shapes=[
            vmem((SRC, TOK, WIDE), BF16),
            vmem((2, 4, 2, 16, D), BF16),
            vmem((OWN, ROWS, D), BF16),
            vmem((OWN, ROWS, HD), BF16),
            vmem((OWN, ROWS, 128), F32),
            vmem((TOPK * TOK, 2 * HD), BF16),
            vmem((OWN * MAIN, TOPK * TOK), BF16),
            vmem((OWN * MAIN, TOPK * TOK), BF16),
            vmem((OWN * MAIN, SRC * TOK), BF16),
            vmem((OWN * MAIN, 2 * HD), F32),
            vmem((OWN, 4, 32, D), BF16),
            vmem((OWN, 2, 32, HALF), BF16),
            vmem((OWN, 2, 32, D), BF16),
            vmem((OWN, 2, 32, HALF), BF16),
            vmem((FAR, 16, D), F32),
            vmem((FAR - 1, 16, D), F32),
            vmem((2 * OWN, 16, D), F32),
            vmem((SRC, ROWS, 2 * HD), BF16),
            vmem((OWN * MAIN, 2 * HD), BF16),
            sems((SRC,)),
            sems((2,)),
            sems((OWN, 4)),
            sems((OWN, 4)),
            sems((OWN, 2)),
            sems((OWN, 2)),
            sems((2 * OWN,)),
            sems((FAR,)),
            sems((FAR - 1,)),
            sems,
            sems((SRC,)),
            sems((SRC,)),
            sems,
        ],
        compiler_params=pltpu.CompilerParams(
            collective_id=1, has_side_effects=True, vmem_limit_bytes=67043328
        ),
    )(tokens, weights)


def return_kernel(routes_ref, back_ref, head_ref, gate_ref):
    routes = routes_ref[...]
    experts = lax.broadcasted_iota(jnp.int32, (TOK, 128), 1)
    named = [(routes[:, k : k + 1] == experts).astype(F32) for k in range(TOPK)]
    chosen = functools.reduce(lambda a, b: a + b, named)
    lower = (iota((TOK, TOK), 1) < iota((TOK, TOK), 0)).astype(BF16)
    before = jnp.dot(lower, chosen.astype(BF16), preferred_element_type=F32)
    rows = lax.broadcasted_iota(jnp.int32, (TOK, SRC * ROWS), 1)
    gates = jnp.zeros((TOK, 128), F32)
    for k in range(TOPK):
        expert = routes[:, k : k + 1]
        slot = jnp.sum(named[k] * before, axis=1, keepdims=True).astype(jnp.int32)
        owner = 2 * (expert >> 4) + (expert & 1)
        index = (expert & 15) >> 1
        place = jnp.where(
            slot < MAIN, index * MAIN + slot, OWN * MAIN + OVER * index + slot - MAIN
        )
        pick = (rows == owner * ROWS + place).astype(F32).astype(BF16)
        block = jnp.dot(pick, back_ref[...], preferred_element_type=F32)
        head_ref[:, k * HD : (k + 1) * HD] = block[:, 0:HD].astype(BF16)
        gates = jnp.where(experts == k, block[:, HD:], gates)
    gate_ref[...] = gates[:, 0:TOPK].astype(BF16)


def put_back(routes, back):
    return pl.pallas_call(
        return_kernel,
        out_shape=(
            jax.ShapeDtypeStruct((TOK, TOPK * HD), BF16),
            jax.ShapeDtypeStruct((TOK, TOPK), BF16),
        ),
        compiler_params=pltpu.CompilerParams(vmem_limit_bytes=32 << 20),
    )(routes, back)


def local(head_outputs, out_grad, gate_weights, route_ids, out_proj):
    packed = jnp.concatenate(
        [
            out_grad,
            head_outputs.reshape(TOK, TOPK * HD),
            gate_weights,
            route_ids.astype(BF16),
            jnp.zeros((TOK, 128 - 2 * TOPK), BF16),
        ],
        axis=1,
    )
    tokens = lax.all_gather(packed, "dp")
    weights = gather_weights(out_proj[0])
    grad_proj, got = owner_work(tokens, weights.reshape(4, OWN, 2, 16, D))
    grad_head, grad_gate = put_back(route_ids, got.reshape(SRC * ROWS, 2 * HD))
    return grad_head.reshape(TOK, TOPK, HD), grad_gate, grad_proj[None]


def solution(mesh):
    return jax.shard_map(
        local,
        mesh=mesh,
        in_specs=(
            P(("dp", "expert"), None, None),
            P(("dp", "expert"), None),
            P(("dp", "expert"), None),
            P(("dp", "expert"), None),
            P("expert", None, None),
        ),
        out_specs=(
            P(("dp", "expert"), None, None),
            P(("dp", "expert"), None),
            P("expert", "dp", None),
        ),
        check_vma=False,
    )
```

```python
import functools

import jax
import jax.numpy as jnp
from jax import lax
from jax.experimental import pallas as pl
from jax.experimental.pallas import tpu as pltpu
from jax.sharding import PartitionSpec as P

CAP = 1.5
F32 = jnp.float32
BF16 = jnp.bfloat16

SRC = 8
OWN = 8
TOK = 128
TOPK = 8
HD = 128
D = 4096
MAIN = 16
OVER = 2
ROWS = SRC * (MAIN + OVER)
STEP = 512


def iota(shape, axis):
    return lax.broadcasted_iota(jnp.int32, shape, axis).astype(F32)


def dispatch_source(base, s, xg, xs, gx, gh, gg, hcat, qm, qo, po, over):
    upper = (iota((TOK, TOK), 0) < iota((TOK, TOK), 1)).astype(BF16)
    lane = iota((TOK, 128), 1)
    slot = iota((MAIN, TOK), 0)
    meta = xs[s, :, TOPK * HD :].astype(F32)
    routes = meta.T[TOPK : 2 * TOPK, :]
    named = [(routes == (base + 2 * j).astype(F32)).astype(F32) for j in range(OWN)]
    chosen = jnp.concatenate([jnp.sum(n, axis=0, keepdims=True) for n in named], axis=0)
    before = jnp.dot(chosen.astype(BF16), upper, preferred_element_type=F32)
    shift = (OVER * s - MAIN).astype(F32)
    columns = pl.ds(pl.multiple_of(s * TOK, TOK), TOK)
    picks = []
    for j in range(OWN):
        rows = slice(j * MAIN, (j + 1) * MAIN)
        pos = before[j : j + 1, :]
        spot = jnp.where(chosen[j : j + 1, :] > 0, pos, -1.0)
        picks.append((spot == slot).astype(F32))
        tardy = jnp.where(spot >= MAIN, spot + shift, -1.0)
        po[rows, columns] = (tardy == slot).astype(F32).astype(BF16)
        own = jnp.where(named[j] > 0, pos, -1.0)
        own_tardy = jnp.where(own >= MAIN, own + shift, -1.0)
        for k in range(TOPK):
            piece = slice(k * TOK, (k + 1) * TOK)
            qm[rows, piece] = (own[k : k + 1, :] == slot).astype(F32).astype(BF16)
            qo[rows, piece] = (own_tardy[k : k + 1, :] == slot).astype(F32).astype(BF16)
    pick = jnp.concatenate(picks, axis=0).astype(BF16)
    for k in range(TOPK):
        piece = slice(k * TOK, (k + 1) * TOK)
        hcat[piece, 0:HD] = xs[s, :, k * HD : (k + 1) * HD]
        hcat[piece, HD : 2 * HD] = jnp.where(lane == k, meta, 0.0).astype(BF16)
    out_rows = pl.ds(pl.multiple_of(s * MAIN, MAIN), MAIN)
    for c in range(0, D, STEP):
        block = jnp.dot(pick, xg[s, :, c : c + STEP], preferred_element_type=F32)
        gx[:, out_rows, c : c + STEP] = block.astype(BF16).reshape(OWN, MAIN, STEP)
    block = jnp.dot(qm[...], hcat[...], preferred_element_type=F32)
    gh[:, out_rows, :] = block[:, 0:HD].astype(BF16).reshape(OWN, MAIN, HD)
    gate = jnp.sum(block[:, HD:], axis=1, keepdims=True)
    gg[:, out_rows, :] = jnp.broadcast_to(gate, (OWN * MAIN, 128)).reshape(OWN, MAIN, 128)
    over[...] += jnp.dot(qo[...], hcat[...], preferred_element_type=F32)


def dispatch_rest(xg, gx, gh, gg, po, over):
    tail = slice(SRC * MAIN, ROWS)
    width = 2 * 128
    for c in range(0, D, width):
        tokens = xg[:, :, c : c + width].reshape(SRC * TOK, width)
        block = jnp.dot(po[...], tokens, preferred_element_type=F32)
        gx[:, tail, c : c + width] = block.astype(BF16).reshape(OWN, SRC * OVER, width)
    gh[:, tail, :] = over[:, 0:HD].astype(BF16).reshape(OWN, SRC * OVER, HD)
    gate = jnp.sum(over[:, HD:], axis=1, keepdims=True)
    gg[:, tail, :] = jnp.broadcast_to(gate, (OWN * SRC * OVER, 128)).reshape(OWN, SRC * OVER, 128)


MESH = pl.DeviceIdType.MESH
HALF = D // 2
FAR = 8


def place():
    dp, expert = lax.axis_index("dp"), lax.axis_index("expert")
    y, z = expert // 16, lax.rem(expert, 16)
    x, core = dp // 2, lax.rem(dp, 2)
    odd = lax.rem(z, 2)
    partner = (2 * y + odd, 16 * x + z - odd + core)
    alone = jnp.logical_and(x == y, core == odd)
    return dp, y, z, partner, alone


def meet(peers, partner, alone):
    barrier = pltpu.get_barrier_semaphore()
    for peer in peers:
        pl.semaphore_signal(barrier, inc=1, device_id=peer, device_id_type=MESH)

    @pl.when(jnp.logical_not(alone))
    def _():
        pl.semaphore_signal(barrier, inc=1, device_id=partner, device_id_type=MESH)

    pl.semaphore_wait(barrier, len(peers) + jnp.where(alone, 0, 1))


def send(src, dst, send_sem, recv_sem, device):
    return pltpu.make_async_remote_copy(
        src_ref=src,
        dst_ref=dst,
        send_sem=send_sem,
        recv_sem=recv_sem,
        device_id=device,
        device_id_type=MESH,
    )


def expert_step(i, j, wbuf, slot, gx, gh, gg, part, ret, late):
    heads = gh[j]
    gate = gg[j]
    head_grad = jnp.zeros((ROWS, HD), F32)
    gate_sum = jnp.zeros((ROWS, 128), F32)
    for c in range(0, D, STEP):
        weight = wbuf[slot, :, :, :, c : c + STEP].reshape(HD, STEP)
        pre = jnp.dot(heads, weight, preferred_element_type=F32)
        capped = jnp.tanh(pre * (1.0 / CAP))
        grad = gx[j, :, c : c + STEP].astype(F32)
        grad_capped = grad * capped
        rest = grad - grad_capped * capped
        parts = []
        for b in range(0, STEP, 128):
            gate_sum = gate_sum + grad_capped[:, b : b + 128]
            parts.append((gate * rest[:, b : b + 128]).astype(BF16))
        grad_pre = jnp.concatenate(parts, axis=1)
        head_grad = head_grad + lax.dot_general(
            grad_pre, weight, (((1,), (1,)), ((), ())), preferred_element_type=F32
        )
        grown = lax.dot_general(
            heads, grad_pre, (((0,), (0,)), ((), ())), preferred_element_type=F32
        )
        part[i, :, :, c : c + STEP] = grown.astype(BF16).reshape(4, 32, STEP)
    gate_grad = CAP * jnp.sum(gate_sum, axis=1, keepdims=True)
    both = jnp.concatenate([head_grad, jnp.broadcast_to(gate_grad, (ROWS, 128))], axis=1)
    both = both.astype(BF16)
    rows = pl.ds(pl.multiple_of(j * MAIN, MAIN), MAIN)
    ret[:, rows, :] = both[0 : SRC * MAIN].reshape(SRC, MAIN, 2 * HD)
    late[rows, :] = both[SRC * MAIN :]


def owner_kernel(
    grad_ref, small_ref, proj_ref, out_ref, got_ref, w_ref,
    xg, xs, own, wbuf, gx, gh, gg, hcat, qm, qo, po, over,
    part, a_in, b_in, comb, zl, zr, zout, ret, late,
    mine_sem, ts, tr, own_sem, hold_sem, hs, hr, ys, yr, fs, fr,
    w_sem, ps, pr, cs, cr, zs, zlr, zrr, out_sem, rs, rr, keep_sem,
):
    dp, y, z, partner, alone = place()
    x, core = dp // 2, lax.rem(dp, 2)
    ring = lambda v, step, n: lax.rem(v + step + n, n)
    yu, yd, y2 = ring(y, 1, 4), ring(y, -1, 4), ring(y, 2, 4)
    up, down = (dp, yu * 16 + z), (dp, yd * 16 + z)
    right, left = (dp, y * 16 + ring(z, 1, 16)), (dp, y * 16 + ring(z, -1, 16))
    here = y * 16 + z
    others = [(lax.rem(dp + k, SRC), here) for k in range(1, SRC)]
    base = (dp // 2) * 16 + lax.rem(dp, 2)
    low, high = pl.ds(0, HALF), pl.ds(HALF, HALF)

    group = lambda step, flip: 2 * ring(x, step, 4) + (1 - core if flip else core)
    mine = (
        pltpu.make_async_copy(grad_ref, xg.at[dp], mine_sem.at[0]),
        pltpu.make_async_copy(small_ref, xs.at[dp], mine_sem.at[1]),
    )

    def tokens(n):
        device = (group((1, -1, 1, -1, 0, 0, 0, 0)[n], n >= 4), here)
        origin = group((0, 0, -1, 1, 0, -1, 1, 2)[n], False)
        whole = n in (0, 1, 4, 5, 6, 7)
        first = n in (0, 1, 4)
        wide = grad_ref if first else xg.at[origin]
        narrow = small_ref if first else xs.at[origin]
        to_wide, to_narrow = xg.at[origin], xs.at[origin]
        if not whole:
            half = low if n == 2 else high
            wide, to_wide = xg.at[origin, :, half], xg.at[origin, :, half]
        out = [send(wide, to_wide, ts.at[n, 0], tr.at[n, 0], device)]
        if n != 3:
            out.append(send(narrow, to_narrow, ts.at[n, 1], tr.at[n, 1], device))
        return out

    def start(copies):
        for one in copies:
            one.start()

    def arrive(copies):
        for one in copies:
            one.wait_recv()

    start(mine)
    meet([up, down, right, left] + others, partner, alone)

    slab = proj_ref.at[pl.ds(pl.multiple_of(dp * 16, 16), 16), :]
    trade = send(slab, own, own_sem.at[0], own_sem.at[1], partner)
    local = pltpu.make_async_copy(slab, own, own_sem.at[1])

    @pl.when(alone)
    def _():
        local.start()

    @pl.when(jnp.logical_not(alone))
    def _():
        trade.start()

    for n in (0, 1, 4):
        start(tokens(n))

    @pl.when(alone)
    def _():
        local.wait()

    @pl.when(jnp.logical_not(alone))
    def _():
        trade.wait()

    hold = pltpu.make_async_copy(own, w_ref.at[y, z], hold_sem)
    hold.start()

    def along_z(src, col, way, hop):
        return send(src, w_ref.at[y, col], hs.at[way, hop], hr.at[way, hop], (right, left)[way])

    def along_y(src, col, way):
        return send(src, w_ref.at[y, col], ys.at[way, col], yr.at[way, col], (up, down)[way])

    def forward(row, col, way):
        block = w_ref.at[row, col, :, (low, high)[way]]
        return send(block, block, fs.at[way, col], fr.at[way, col], (up, down)[way])

    along_z(own, z, 0, 0).start()
    along_z(own, z, 1, 0).start()
    along_y(own, z, 0).start()
    along_y(own, z, 1).start()
    for hop in range(1, FAR + 1):
        for way in range(2 if hop < FAR else 1):
            col = ring(z, -hop if way == 0 else hop, 16)
            block = w_ref.at[y, col]
            along_z(block, col, way, hop - 1).wait_recv()
            if hop < FAR - way:
                along_z(block, col, way, hop).start()
            along_y(block, col, 0).start()
            along_y(block, col, 1).start()

    def column(step):
        away = (step + 1) // 2
        return lax.rem(z + 16 + jnp.where(lax.rem(step, 2) == 1, -away, away), 16)

    def pass_on(step, _):
        col = column(step)
        send(own, w_ref.at[yd, col], ys.at[0, col], yr.at[0, col], up).wait_recv()
        forward(yd, col, 0).start()
        send(own, w_ref.at[yu, col], ys.at[1, col], yr.at[1, col], down).wait_recv()
        forward(yu, col, 1).start()
        return 0

    def settle(step, _):
        col = column(step)
        forward(y2, col, 0).wait_recv()
        forward(y2, col, 1).wait_recv()
        return 0

    def expert_at(i):
        away = 4 - (i + 1) // 2
        return lax.rem(z // 2 + OWN + jnp.where(lax.rem(i, 2) == 1, away, -away), OWN)

    def weight_copy(i):
        slot = lax.rem(i, 2)
        pair = w_ref.at[:, pl.ds(2 * expert_at(i), 2)]
        return pltpu.make_async_copy(pair, wbuf.at[slot], w_sem.at[slot])

    arrive(tokens(0))
    start(tokens(2))
    start(tokens(5))
    arrive(tokens(1))
    start(tokens(3))
    start(tokens(6))
    for one in mine:
        one.wait()
    over[...] = jnp.zeros_like(over)

    def one_source(n, _):
        @pl.when(n == 1)
        def _():
            arrive(tokens(4))

        @pl.when(n == 4)
        def _():
            arrive(tokens(5))

        @pl.when(n == 5)
        def _():
            arrive(tokens(6))

        @pl.when(n == 6)
        def _():
            lax.fori_loop(0, 16, pass_on, 0)
            arrive(tokens(2))
            arrive(tokens(3))
            start(tokens(7))

        @pl.when(n == 7)
        def _():
            arrive(tokens(7))

        step = jnp.where(n < 2, 0, jnp.where(n >= 6, 2, jnp.where(lax.rem(n, 2) == 0, -1, 1)))
        flip = (n == 1) | (n == 4) | (n == 5) | (n == 7)
        s = 2 * ring(x, step, 4) + jnp.where(flip, 1 - core, core)
        dispatch_source(base, s, xg, xs, gx, gh, gg, hcat, qm, qo, po, over)
        return 0

    lax.fori_loop(0, SRC, one_source, 0)
    dispatch_rest(xg, gx, gh, gg, po, over)
    lax.fori_loop(0, 16, settle, 0)
    hold.wait()
    weight_copy(0).start()

    def first_sends(i):
        return (
            send(part.at[i, y2, :, low], a_in.at[i, 0], ps.at[i, 0], pr.at[i, 0], up),
            send(part.at[i, y2, :, high], a_in.at[i, 1], ps.at[i, 1], pr.at[i, 1], down),
            send(part.at[i, yu, :, high], b_in.at[i, 0, :, high], ps.at[i, 2], pr.at[i, 2], up),
            send(part.at[i, yd, :, low], b_in.at[i, 1, :, low], ps.at[i, 3], pr.at[i, 3], down),
        )

    def second_sends(i):
        return (
            send(comb.at[i, 0], b_in.at[i, 0, :, low], cs.at[i, 0], cr.at[i, 0], up),
            send(comb.at[i, 1], b_in.at[i, 1, :, high], cs.at[i, 1], cr.at[i, 1], down),
        )

    def combine(i):
        first, second = first_sends(i), second_sends(i)
        first[0].wait_recv()
        comb[i, 0] = (part[i, yu, :, low].astype(F32) + a_in[i, 0].astype(F32)).astype(BF16)
        second[0].start()
        first[1].wait_recv()
        comb[i, 1] = (part[i, yd, :, high].astype(F32) + a_in[i, 1].astype(F32)).astype(BF16)
        second[1].start()

    def to_right(k, slot):
        return send(zout.at[k], zl.at[slot], zs.at[k], zlr.at[slot], right)

    def to_left(k, slot):
        return send(zout.at[k], zr.at[slot], zs.at[k], zrr.at[slot], left)

    def to_partner(k):
        return send(zout.at[k], out_ref, zs.at[k], out_sem, partner)

    def finish(i):
        for one in first_sends(i)[2:] + second_sends(i):
            one.wait_recv()
        total = (
            part[i, y].astype(F32) + b_in[i, 0].astype(F32) + b_in[i, 1].astype(F32)
        )
        for c in range(2):
            zout[2 * i + c] = total[16 * c : 16 * (c + 1)]

    def along(i, lagging):
        j = expert_at(i)
        for c in range(2):
            k = 2 * i + c
            ahead = lax.rem(2 * j + c - z + 16, 16)
            behind = lax.rem(16 - ahead, 16)
            odd = lax.rem(z, 2) == 1
            lag = jnp.where(ahead <= FAR, odd, jnp.logical_not(odd)) | (ahead == 0)
            now = lag if lagging else jnp.logical_not(lag)

            @pl.when(now & (ahead < FAR))
            def _():
                to_right(k, ahead).wait_recv()
                zout[k] += zl[ahead]

            @pl.when(now & (behind < FAR - 1))
            def _():
                to_left(k, behind).wait_recv()
                zout[k] += zr[behind]

            @pl.when(now & (ahead >= 1) & (ahead <= FAR))
            def _():
                to_right(k, ahead - 1).start()

            @pl.when(now & (ahead > FAR))
            def _():
                to_left(k, behind - 1).start()

            @pl.when(now & (ahead == 0) & alone)
            def _():
                pltpu.make_async_copy(zout.at[k], out_ref, zs.at[k]).start()

            @pl.when(now & (ahead == 0) & jnp.logical_not(alone))
            def _():
                to_partner(k).start()

    def returns():
        out = []
        for k in range(1, SRC):
            to = lax.rem(dp + k, SRC)
            out.append(send(ret.at[to], got_ref.at[dp], rs.at[k], rr.at[k], others[k - 1]))
        return out

    keep = pltpu.make_async_copy(ret.at[dp], got_ref.at[dp], keep_sem)

    def one_expert(i, _):
        @pl.when(i < OWN)
        def _():
            @pl.when(i + 1 < OWN)
            def _():
                weight_copy(i + 1).start()

            weight_copy(i).wait()
            expert_step(i, expert_at(i), wbuf, lax.rem(i, 2), gx, gh, gg, part, ret, late)
            for one in first_sends(i):
                one.start()

        @pl.when(i == OWN - 1)
        def _():
            to = lax.broadcasted_iota(jnp.int32, (OWN * MAIN, OWN * MAIN), 0)
            source = lax.broadcasted_iota(jnp.int32, (OWN * MAIN, OWN * MAIN), 1)
            want = (lax.rem(to, 16) // 2) * 16 + (to // 16) * 2 + lax.rem(to, 2)
            shuffle = (source == want).astype(F32).astype(BF16)
            moved = jnp.dot(shuffle, late[...], preferred_element_type=F32).astype(BF16)
            ret[:, OWN * MAIN :, :] = moved.reshape(SRC, OWN * OVER, 2 * HD)
            for one in returns():
                one.start()
            keep.start()

        @pl.when(jnp.logical_and(i >= 1, i <= OWN))
        def _():
            combine(i - 1)

        @pl.when(jnp.logical_and(i >= 2, i <= OWN + 1))
        def _():
            finish(i - 2)
            along(i - 2, False)

        @pl.when(i >= 3)
        def _():
            along(i - 3, True)

        return 0

    lax.fori_loop(0, OWN + 3, one_expert, 0)
    for one in returns():
        one.wait()
    keep.wait()

    @pl.when(jnp.logical_not(alone))
    def _():
        to_partner(0).wait_recv()

    def drain(i, _):
        for one in first_sends(i) + second_sends(i):
            one.wait_send()
        to_right(2 * i, 0).wait_send()
        to_right(2 * i + 1, 0).wait_send()
        return 0

    lax.fori_loop(0, OWN, drain, 0)
    for n in range(8):
        for one in tokens(n):
            one.wait_send()
    for hop in range(FAR):
        for way in range(2):
            if hop < FAR - way:
                along_z(own, z, way, hop).wait_send()

    def drain_y(col, _):
        for way in range(2):
            along_y(own, col, way).wait_send()
            forward(y2, col, way).wait_send()
        return 0

    lax.fori_loop(0, 16, drain_y, 0)


def owner_work(grads, small, proj):
    sems = pltpu.SemaphoreType.DMA
    vmem = pltpu.VMEM
    return pl.pallas_call(
        owner_kernel,
        out_shape=(
            jax.ShapeDtypeStruct((16, D), F32),
            jax.ShapeDtypeStruct((SRC, ROWS, 2 * HD), BF16),
            jax.ShapeDtypeStruct((4, 16, 16, D), BF16),
        ),
        in_specs=[pl.BlockSpec(memory_space=pl.ANY)] * 3,
        out_specs=(pl.BlockSpec(memory_space=pl.ANY),) * 3,
        scratch_shapes=[
            vmem((SRC, TOK, D), BF16),
            vmem((SRC, TOK, TOPK * HD + 128), BF16),
            vmem((16, D), BF16),
            vmem((2, 4, 2, 16, D), BF16),
            vmem((OWN, ROWS, D), BF16),
            vmem((OWN, ROWS, HD), BF16),
            vmem((OWN, ROWS, 128), F32),
            vmem((TOPK * TOK, 2 * HD), BF16),
            vmem((OWN * MAIN, TOPK * TOK), BF16),
            vmem((OWN * MAIN, TOPK * TOK), BF16),
            vmem((OWN * MAIN, SRC * TOK), BF16),
            vmem((OWN * MAIN, 2 * HD), F32),
            vmem((OWN, 4, 32, D), BF16),
            vmem((OWN, 2, 32, HALF), BF16),
            vmem((OWN, 2, 32, D), BF16),
            vmem((OWN, 2, 32, HALF), BF16),
            vmem((FAR, 16, D), F32),
            vmem((FAR - 1, 16, D), F32),
            vmem((2 * OWN, 16, D), F32),
            vmem((SRC, ROWS, 2 * HD), BF16),
            vmem((OWN * MAIN, 2 * HD), BF16),
            sems((2,)),
            sems((8, 2)),
            sems((8, 2)),
            sems((2,)),
            sems,
            sems((2, FAR)),
            sems((2, FAR)),
            sems((2, 16)),
            sems((2, 16)),
            sems((2, 16)),
            sems((2, 16)),
            sems((2,)),
            sems((OWN, 4)),
            sems((OWN, 4)),
            sems((OWN, 2)),
            sems((OWN, 2)),
            sems((2 * OWN,)),
            sems((FAR,)),
            sems((FAR - 1,)),
            sems,
            sems((SRC,)),
            sems((SRC,)),
            sems,
        ],
        compiler_params=pltpu.CompilerParams(
            collective_id=0, has_side_effects=True, vmem_limit_bytes=67043328
        ),
    )(grads, small, proj)


def return_kernel(routes_ref, back_ref, head_ref, gate_ref):
    routes = routes_ref[...]
    experts = lax.broadcasted_iota(jnp.int32, (TOK, 128), 1)
    named = [(routes[:, k : k + 1] == experts).astype(F32) for k in range(TOPK)]
    chosen = functools.reduce(lambda a, b: a + b, named)
    lower = (iota((TOK, TOK), 1) < iota((TOK, TOK), 0)).astype(BF16)
    before = jnp.dot(lower, chosen.astype(BF16), preferred_element_type=F32)
    rows = lax.broadcasted_iota(jnp.int32, (TOK, SRC * ROWS), 1)
    gates = jnp.zeros((TOK, 128), F32)
    for k in range(TOPK):
        expert = routes[:, k : k + 1]
        slot = jnp.sum(named[k] * before, axis=1, keepdims=True).astype(jnp.int32)
        owner = 2 * (expert >> 4) + (expert & 1)
        index = (expert & 15) >> 1
        place = jnp.where(
            slot < MAIN, index * MAIN + slot, OWN * MAIN + OVER * index + slot - MAIN
        )
        pick = (rows == owner * ROWS + place).astype(F32).astype(BF16)
        block = jnp.dot(pick, back_ref[...], preferred_element_type=F32)
        head_ref[:, k * HD : (k + 1) * HD] = block[:, 0:HD].astype(BF16)
        gates = jnp.where(experts == k, block[:, HD:], gates)
    gate_ref[...] = gates[:, 0:TOPK].astype(BF16)


def put_back(routes, back):
    return pl.pallas_call(
        return_kernel,
        out_shape=(
            jax.ShapeDtypeStruct((TOK, TOPK * HD), BF16),
            jax.ShapeDtypeStruct((TOK, TOPK), BF16),
        ),
        compiler_params=pltpu.CompilerParams(vmem_limit_bytes=32 << 20),
    )(routes, back)


def local(head_outputs, out_grad, gate_weights, route_ids, out_proj):
    small = jnp.concatenate(
        [
            head_outputs.reshape(TOK, TOPK * HD),
            gate_weights,
            route_ids.astype(BF16),
            jnp.zeros((TOK, 128 - 2 * TOPK), BF16),
        ],
        axis=1,
    )
    grad_proj, got, _ = owner_work(out_grad, small, out_proj[0])
    grad_head, grad_gate = put_back(route_ids, got.reshape(SRC * ROWS, 2 * HD))
    return grad_head.reshape(TOK, TOPK, HD), grad_gate, grad_proj[None]


def solution(mesh):
    return jax.shard_map(
        local,
        mesh=mesh,
        in_specs=(
            P(("dp", "expert"), None, None),
            P(("dp", "expert"), None),
            P(("dp", "expert"), None),
            P(("dp", "expert"), None),
            P("expert", None, None),
        ),
        out_specs=(
            P(("dp", "expert"), None, None),
            P(("dp", "expert"), None),
            P("expert", "dp", None),
        ),
        check_vma=False,
    )
```

```python
import functools

import jax
import jax.numpy as jnp
from jax import lax
from jax.experimental import pallas as pl
from jax.experimental.pallas import tpu as pltpu
from jax.sharding import PartitionSpec as P

CAP = 1.5
F32 = jnp.float32
BF16 = jnp.bfloat16

SRC = 8
OWN = 8
TOK = 128
TOPK = 8
HD = 128
D = 4096
MAIN = 16
OVER = 2
ROWS = SRC * (MAIN + OVER)
STEP = 512


def iota(shape, axis):
    return lax.broadcasted_iota(jnp.int32, shape, axis).astype(F32)


def dispatch_source(base, s, xg, xs, gx, gh, gg, hcat, qm, qo, po, over):
    upper = (iota((TOK, TOK), 0) < iota((TOK, TOK), 1)).astype(BF16)
    lane = iota((TOK, 128), 1)
    slot = iota((MAIN, TOK), 0)
    meta = xs[s, :, TOPK * HD :].astype(F32)
    routes = meta.T[TOPK : 2 * TOPK, :]
    named = [(routes == (base + 2 * j).astype(F32)).astype(F32) for j in range(OWN)]
    chosen = jnp.concatenate([jnp.sum(n, axis=0, keepdims=True) for n in named], axis=0)
    before = jnp.dot(chosen.astype(BF16), upper, preferred_element_type=F32)
    shift = (OVER * s - MAIN).astype(F32)
    columns = pl.ds(pl.multiple_of(s * TOK, TOK), TOK)
    picks = []
    for j in range(OWN):
        rows = slice(j * MAIN, (j + 1) * MAIN)
        pos = before[j : j + 1, :]
        spot = jnp.where(chosen[j : j + 1, :] > 0, pos, -1.0)
        picks.append((spot == slot).astype(F32))
        tardy = jnp.where(spot >= MAIN, spot + shift, -1.0)
        po[rows, columns] = (tardy == slot).astype(F32).astype(BF16)
        own = jnp.where(named[j] > 0, pos, -1.0)
        own_tardy = jnp.where(own >= MAIN, own + shift, -1.0)
        for k in range(TOPK):
            piece = slice(k * TOK, (k + 1) * TOK)
            qm[rows, piece] = (own[k : k + 1, :] == slot).astype(F32).astype(BF16)
            qo[rows, piece] = (own_tardy[k : k + 1, :] == slot).astype(F32).astype(BF16)
    pick = jnp.concatenate(picks, axis=0).astype(BF16)
    for k in range(TOPK):
        piece = slice(k * TOK, (k + 1) * TOK)
        hcat[piece, 0:HD] = xs[s, :, k * HD : (k + 1) * HD]
        hcat[piece, HD : 2 * HD] = jnp.where(lane == k, meta, 0.0).astype(BF16)
    out_rows = pl.ds(pl.multiple_of(s * MAIN, MAIN), MAIN)
    for c in range(0, D, STEP):
        block = jnp.dot(pick, xg[s, :, c : c + STEP], preferred_element_type=F32)
        gx[:, out_rows, c : c + STEP] = block.astype(BF16).reshape(OWN, MAIN, STEP)
    block = jnp.dot(qm[...], hcat[...], preferred_element_type=F32)
    gh[:, out_rows, :] = block[:, 0:HD].astype(BF16).reshape(OWN, MAIN, HD)
    gate = jnp.sum(block[:, HD:], axis=1, keepdims=True)
    gg[:, out_rows, :] = jnp.broadcast_to(gate, (OWN * MAIN, 128)).reshape(OWN, MAIN, 128)
    over[...] += jnp.dot(qo[...], hcat[...], preferred_element_type=F32)


def dispatch_rest(xg, gx, gh, gg, po, over):
    tail = slice(SRC * MAIN, ROWS)
    width = 2 * 128
    for c in range(0, D, width):
        tokens = xg[:, :, c : c + width].reshape(SRC * TOK, width)
        block = jnp.dot(po[...], tokens, preferred_element_type=F32)
        gx[:, tail, c : c + width] = block.astype(BF16).reshape(OWN, SRC * OVER, width)
    gh[:, tail, :] = over[:, 0:HD].astype(BF16).reshape(OWN, SRC * OVER, HD)
    gate = jnp.sum(over[:, HD:], axis=1, keepdims=True)
    gg[:, tail, :] = jnp.broadcast_to(gate, (OWN * SRC * OVER, 128)).reshape(OWN, SRC * OVER, 128)


MESH = pl.DeviceIdType.MESH
HALF = D // 2
ZFIRST = 2816
FAR = 8


def place():
    dp, expert = lax.axis_index("dp"), lax.axis_index("expert")
    y, z = expert // 16, lax.rem(expert, 16)
    x, core = dp // 2, lax.rem(dp, 2)
    odd = lax.rem(z, 2)
    partner = (2 * y + odd, 16 * x + z - odd + core)
    alone = jnp.logical_and(x == y, core == odd)
    return dp, y, z, partner, alone


def meet(peers, partner, alone):
    barrier = pltpu.get_barrier_semaphore()
    for peer in peers:
        pl.semaphore_signal(barrier, inc=1, device_id=peer, device_id_type=MESH)

    @pl.when(jnp.logical_not(alone))
    def _():
        pl.semaphore_signal(barrier, inc=1, device_id=partner, device_id_type=MESH)

    pl.semaphore_wait(barrier, len(peers) + jnp.where(alone, 0, 1))


def send(src, dst, send_sem, recv_sem, device):
    return pltpu.make_async_remote_copy(
        src_ref=src,
        dst_ref=dst,
        send_sem=send_sem,
        recv_sem=recv_sem,
        device_id=device,
        device_id_type=MESH,
    )


def expert_step(i, j, wbuf, slot, gx, gh, gg, part, ret, late):
    heads = gh[j]
    gate = gg[j]
    head_grad = jnp.zeros((ROWS, HD), F32)
    gate_sum = jnp.zeros((ROWS, 128), F32)
    for c in range(0, D, STEP):
        weight = wbuf[slot, :, :, :, c : c + STEP].reshape(HD, STEP)
        pre = jnp.dot(heads, weight, preferred_element_type=F32)
        capped = jnp.tanh(pre * (1.0 / CAP))
        grad = gx[j, :, c : c + STEP].astype(F32)
        grad_capped = grad * capped
        rest = grad - grad_capped * capped
        parts = []
        for b in range(0, STEP, 128):
            gate_sum = gate_sum + grad_capped[:, b : b + 128]
            parts.append((gate * rest[:, b : b + 128]).astype(BF16))
        grad_pre = jnp.concatenate(parts, axis=1)
        head_grad = head_grad + lax.dot_general(
            grad_pre, weight, (((1,), (1,)), ((), ())), preferred_element_type=F32
        )
        grown = lax.dot_general(
            heads, grad_pre, (((0,), (0,)), ((), ())), preferred_element_type=F32
        )
        part[i, :, :, c : c + STEP] = grown.astype(BF16).reshape(4, 32, STEP)
    gate_grad = CAP * jnp.sum(gate_sum, axis=1, keepdims=True)
    both = jnp.concatenate([head_grad, jnp.broadcast_to(gate_grad, (ROWS, 128))], axis=1)
    both = both.astype(BF16)
    rows = pl.ds(pl.multiple_of(j * MAIN, MAIN), MAIN)
    ret[:, rows, :] = both[0 : SRC * MAIN].reshape(SRC, MAIN, 2 * HD)
    late[rows, :] = both[SRC * MAIN :]


def owner_kernel(
    grad_ref, small_ref, proj_ref, out_ref, got_ref, w_ref,
    xg, xs, own, wbuf, gx, gh, gg, hcat, qm, qo, po, over,
    part, a_in, b_in, comb, zl, zr, zout, ret, late,
    mine_sem, ts, tr, own_sem, hold_sem, hs, hr, ys, yr, fs, fr, es, er, bs, br,
    w_sem, ps, pr, cs, cr, zs, zlr, zrr, out_sem, rs, rr, keep_sem,
):
    dp, y, z, partner, alone = place()
    x, core = dp // 2, lax.rem(dp, 2)
    ring = lambda v, step, n: lax.rem(v + step + n, n)
    yu, yd, y2 = ring(y, 1, 4), ring(y, -1, 4), ring(y, 2, 4)
    up, down = (dp, yu * 16 + z), (dp, yd * 16 + z)
    right, left = (dp, y * 16 + ring(z, 1, 16)), (dp, y * 16 + ring(z, -1, 16))
    here = y * 16 + z
    others = [(lax.rem(dp + k, SRC), here) for k in range(1, SRC)]
    base = (dp // 2) * 16 + lax.rem(dp, 2)
    low, high = pl.ds(0, HALF), pl.ds(HALF, HALF)

    group = lambda step, flip: 2 * ring(x, step, 4) + (1 - core if flip else core)
    mine = (
        pltpu.make_async_copy(grad_ref, xg.at[dp], mine_sem.at[0]),
        pltpu.make_async_copy(small_ref, xs.at[dp], mine_sem.at[1]),
    )

    def tokens(n):
        device = (group((1, -1, 1, -1, 0, 0, 0, 0)[n], n >= 4), here)
        origin = group((0, 0, -1, 1, 0, -1, 1, 2)[n], False)
        whole = n in (0, 1, 4, 5, 6, 7)
        first = n in (0, 1, 4)
        wide = grad_ref if first else xg.at[origin]
        narrow = small_ref if first else xs.at[origin]
        to_wide, to_narrow = xg.at[origin], xs.at[origin]
        if not whole:
            half = low if n == 2 else high
            wide, to_wide = xg.at[origin, :, half], xg.at[origin, :, half]
        out = [send(wide, to_wide, ts.at[n, 0], tr.at[n, 0], device)]
        if n != 3:
            out.append(send(narrow, to_narrow, ts.at[n, 1], tr.at[n, 1], device))
        return out

    def start(copies):
        for one in copies:
            one.start()

    def arrive(copies):
        for one in copies:
            one.wait_recv()

    start(mine)
    meet([up, down, right, left] + others, partner, alone)

    slab = proj_ref.at[pl.ds(pl.multiple_of(dp * 16, 16), 16), :]
    trade = send(slab, own, own_sem.at[0], own_sem.at[1], partner)
    local = pltpu.make_async_copy(slab, own, own_sem.at[1])

    @pl.when(alone)
    def _():
        local.start()

    @pl.when(jnp.logical_not(alone))
    def _():
        trade.start()

    for n in (0, 1, 4):
        start(tokens(n))

    @pl.when(alone)
    def _():
        local.wait()

    @pl.when(jnp.logical_not(alone))
    def _():
        trade.wait()

    hold = pltpu.make_async_copy(own, w_ref.at[y, z], hold_sem)
    hold.start()

    zcols = pl.ds(0, ZFIRST)
    ycols = pl.ds(ZFIRST, D - ZFIRST)
    zhalf = (pl.ds(0, ZFIRST // 2), pl.ds(ZFIRST // 2, ZFIRST // 2))
    yhalf = (pl.ds(ZFIRST, (D - ZFIRST) // 2), pl.ds((D + ZFIRST) // 2, (D - ZFIRST) // 2))

    def along_z(src, col, way, hop):
        to = w_ref.at[y, col, :, zcols]
        return send(src, to, hs.at[way, hop], hr.at[way, hop], (right, left)[way])

    def along_y(src, col, way):
        to = w_ref.at[y, col, :, zcols]
        return send(src, to, ys.at[way, col], yr.at[way, col], (up, down)[way])

    def forward(row, col, way):
        block = w_ref.at[row, col, :, zhalf[way]]
        return send(block, block, fs.at[way, col], fr.at[way, col], (up, down)[way])

    def early_y(way):
        to = w_ref.at[y, z, :, ycols]
        return send(own.at[:, ycols], to, es.at[way], er.at[way], (up, down)[way])

    def early_forward(row, way):
        block = w_ref.at[row, z, :, yhalf[way]]
        return send(block, block, es.at[2 + way], er.at[2 + way], (up, down)[way])

    def bundle(col, way, hop):
        block = w_ref.at[:, col, :, ycols]
        return send(block, block, bs.at[way, hop], br.at[way, hop], (right, left)[way])

    mine_z = own.at[:, zcols]
    early_y(0).start()
    early_y(1).start()
    along_z(mine_z, z, 0, 0).start()
    along_z(mine_z, z, 1, 0).start()
    along_y(mine_z, z, 0).start()
    along_y(mine_z, z, 1).start()
    early_y(0).wait_recv()
    early_forward(yd, 0).start()
    early_y(1).wait_recv()
    early_forward(yu, 1).start()

    def column(step):
        away = (step + 1) // 2
        return lax.rem(z + 16 + jnp.where(lax.rem(step, 2) == 1, -away, away), 16)

    def pass_on(step):
        col = column(step)
        along_y(mine_z, col, 0).wait_recv()
        forward(yd, col, 0).start()
        along_y(mine_z, col, 1).wait_recv()
        forward(yu, col, 1).start()

    def settle(step, _):
        col = column(step)
        forward(y2, col, 0).wait_recv()
        forward(y2, col, 1).wait_recv()
        return 0

    def arrived_z(hop, way):
        col = ring(z, -hop if way == 0 else hop, 16)
        block = w_ref.at[y, col, :, zcols]
        along_z(block, col, way, hop - 1).wait_recv()

        @pl.when(hop < FAR - way)
        def _():
            along_z(block, col, way, hop).start()

        along_y(block, col, 0).start()
        along_y(block, col, 1).start()

    def arrived_bundle(hop, way):
        col = ring(z, -hop if way == 0 else hop, 16)
        bundle(col, way, hop - 1).wait_recv()

        @pl.when(hop < FAR - way)
        def _():
            bundle(col, way, hop).start()

    def expert_at(i):
        away = 4 - (i + 1) // 2
        return lax.rem(z // 2 + OWN + jnp.where(lax.rem(i, 2) == 1, away, -away), OWN)

    def weight_copy(i):
        slot = lax.rem(i, 2)
        pair = w_ref.at[:, pl.ds(2 * expert_at(i), 2)]
        return pltpu.make_async_copy(pair, wbuf.at[slot], w_sem.at[slot])

    over[...] = jnp.zeros_like(over)

    def gather_step(hop, _):
        @pl.when(hop <= FAR)
        def _():
            arrived_z(hop, 0)

        @pl.when(hop < FAR)
        def _():
            arrived_z(hop, 1)

        @pl.when(hop == 1)
        def _():
            early_forward(y2, 0).wait_recv()
            early_forward(y2, 1).wait_recv()
            hold.wait()
            bundle(z, 0, 0).start()
            bundle(z, 1, 0).start()

        @pl.when((hop >= 2) & (hop <= FAR + 1))
        def _():
            arrived_bundle(hop - 1, 0)

        @pl.when((hop >= 2) & (hop <= FAR))
        def _():
            arrived_bundle(hop - 1, 1)

        @pl.when(hop == 2)
        def _():
            pass_on(0)

        @pl.when(hop >= 3)
        def _():
            pass_on(2 * (hop - 2) - 1)

        @pl.when((hop >= 3) & (hop < FAR + 2))
        def _():
            pass_on(2 * (hop - 2))

        n = hop - 3

        @pl.when(n == 0)
        def _():
            for one in mine:
                one.wait()

        @pl.when(n == 1)
        def _():
            arrive(tokens(4))

        @pl.when(n == 2)
        def _():
            arrive(tokens(0))
            start(tokens(2))
            start(tokens(5))
            arrive(tokens(1))
            start(tokens(3))
            start(tokens(6))

        @pl.when(n == 4)
        def _():
            arrive(tokens(5))

        @pl.when(n == 5)
        def _():
            arrive(tokens(6))

        @pl.when(n == 6)
        def _():
            arrive(tokens(2))
            arrive(tokens(3))
            start(tokens(7))

        @pl.when(n == 7)
        def _():
            arrive(tokens(7))

        @pl.when(n >= 0)
        def _():
            step = jnp.where(n < 2, 0, jnp.where(n >= 6, 2, jnp.where(lax.rem(n, 2) == 0, -1, 1)))
            flip = (n == 1) | (n == 4) | (n == 5) | (n == 7)
            s = 2 * ring(x, step, 4) + jnp.where(flip, 1 - core, core)
            dispatch_source(base, s, xg, xs, gx, gh, gg, hcat, qm, qo, po, over)

        return 0

    with jax.named_scope("gather"):
        lax.fori_loop(1, FAR + 3, gather_step, 0)
    with jax.named_scope("rest"):
        dispatch_rest(xg, gx, gh, gg, po, over)
    with jax.named_scope("settle"):
        lax.fori_loop(0, 16, settle, 0)
    weight_copy(0).start()

    def first_sends(i):
        return (
            send(part.at[i, y2, :, low], a_in.at[i, 0], ps.at[i, 0], pr.at[i, 0], up),
            send(part.at[i, y2, :, high], a_in.at[i, 1], ps.at[i, 1], pr.at[i, 1], down),
            send(part.at[i, yu, :, high], b_in.at[i, 0, :, high], ps.at[i, 2], pr.at[i, 2], up),
            send(part.at[i, yd, :, low], b_in.at[i, 1, :, low], ps.at[i, 3], pr.at[i, 3], down),
        )

    def second_sends(i):
        return (
            send(comb.at[i, 0], b_in.at[i, 0, :, low], cs.at[i, 0], cr.at[i, 0], up),
            send(comb.at[i, 1], b_in.at[i, 1, :, high], cs.at[i, 1], cr.at[i, 1], down),
        )

    def combine(i):
        first, second = first_sends(i), second_sends(i)
        first[0].wait_recv()
        comb[i, 0] = (part[i, yu, :, low].astype(F32) + a_in[i, 0].astype(F32)).astype(BF16)
        second[0].start()
        first[1].wait_recv()
        comb[i, 1] = (part[i, yd, :, high].astype(F32) + a_in[i, 1].astype(F32)).astype(BF16)
        second[1].start()

    def to_right(k, slot):
        return send(zout.at[k], zl.at[slot], zs.at[k], zlr.at[slot], right)

    def to_left(k, slot):
        return send(zout.at[k], zr.at[slot], zs.at[k], zrr.at[slot], left)

    def to_partner(k):
        return send(zout.at[k], out_ref, zs.at[k], out_sem, partner)

    def finish(i):
        for one in first_sends(i)[2:] + second_sends(i):
            one.wait_recv()
        total = (
            part[i, y].astype(F32) + b_in[i, 0].astype(F32) + b_in[i, 1].astype(F32)
        )
        for c in range(2):
            zout[2 * i + c] = total[16 * c : 16 * (c + 1)]

    def along(i, lagging):
        j = expert_at(i)
        for c in range(2):
            k = 2 * i + c
            ahead = lax.rem(2 * j + c - z + 16, 16)
            behind = lax.rem(16 - ahead, 16)
            odd = lax.rem(z, 2) == 1
            lag = jnp.where(ahead <= FAR, odd, jnp.logical_not(odd)) | (ahead == 0)
            now = lag if lagging else jnp.logical_not(lag)

            @pl.when(now & (ahead < FAR))
            def _():
                to_right(k, ahead).wait_recv()
                zout[k] += zl[ahead]

            @pl.when(now & (behind < FAR - 1))
            def _():
                to_left(k, behind).wait_recv()
                zout[k] += zr[behind]

            @pl.when(now & (ahead >= 1) & (ahead <= FAR))
            def _():
                to_right(k, ahead - 1).start()

            @pl.when(now & (ahead > FAR))
            def _():
                to_left(k, behind - 1).start()

            @pl.when(now & (ahead == 0) & alone)
            def _():
                pltpu.make_async_copy(zout.at[k], out_ref, zs.at[k]).start()

            @pl.when(now & (ahead == 0) & jnp.logical_not(alone))
            def _():
                to_partner(k).start()

    def returns():
        out = []
        for k in range(1, SRC):
            to = lax.rem(dp + k, SRC)
            out.append(send(ret.at[to], got_ref.at[dp], rs.at[k], rr.at[k], others[k - 1]))
        return out

    keep = pltpu.make_async_copy(ret.at[dp], got_ref.at[dp], keep_sem)

    def one_expert(i, _):
        @pl.when(i < OWN)
        def _():
            @pl.when(i + 1 < OWN)
            def _():
                weight_copy(i + 1).start()

            weight_copy(i).wait()
            with jax.named_scope("expert"):
                expert_step(i, expert_at(i), wbuf, lax.rem(i, 2), gx, gh, gg, part, ret, late)
            for one in first_sends(i):
                one.start()

        @pl.when(i == OWN - 1)
        def _():
            to = lax.broadcasted_iota(jnp.int32, (OWN * MAIN, OWN * MAIN), 0)
            source = lax.broadcasted_iota(jnp.int32, (OWN * MAIN, OWN * MAIN), 1)
            want = (lax.rem(to, 16) // 2) * 16 + (to // 16) * 2 + lax.rem(to, 2)
            shuffle = (source == want).astype(F32).astype(BF16)
            moved = jnp.dot(shuffle, late[...], preferred_element_type=F32).astype(BF16)
            ret[:, OWN * MAIN :, :] = moved.reshape(SRC, OWN * OVER, 2 * HD)
            for one in returns():
                one.start()
            keep.start()

        @pl.when(jnp.logical_and(i >= 1, i <= OWN))
        def _():
            with jax.named_scope("combine"):
                combine(i - 1)

        @pl.when(jnp.logical_and(i >= 2, i <= OWN + 1))
        def _():
            with jax.named_scope("finish"):
                finish(i - 2)
            with jax.named_scope("along"):
                along(i - 2, False)

        @pl.when(i >= 3)
        def _():
            with jax.named_scope("lagging"):
                along(i - 3, True)

        return 0

    lax.fori_loop(0, OWN + 3, one_expert, 0)
    with jax.named_scope("returned"):
        for one in returns():
            one.wait()
        keep.wait()

    @pl.when(jnp.logical_not(alone))
    def _():
        to_partner(0).wait_recv()

    def drain(i, _):
        for one in first_sends(i) + second_sends(i):
            one.wait_send()
        to_right(2 * i, 0).wait_send()
        to_right(2 * i + 1, 0).wait_send()
        return 0

    lax.fori_loop(0, OWN, drain, 0)
    for n in range(8):
        for one in tokens(n):
            one.wait_send()
    for hop in range(FAR):
        for way in range(2):
            if hop < FAR - way:
                along_z(mine_z, z, way, hop).wait_send()
                bundle(z, way, hop).wait_send()
    for way in range(2):
        early_y(way).wait_send()
        early_forward(y2, way).wait_send()

    def drain_y(col, _):
        for way in range(2):
            along_y(mine_z, col, way).wait_send()
            forward(y2, col, way).wait_send()
        return 0

    lax.fori_loop(0, 16, drain_y, 0)


def owner_work(grads, small, proj):
    sems = pltpu.SemaphoreType.DMA
    vmem = pltpu.VMEM
    return pl.pallas_call(
        owner_kernel,
        out_shape=(
            jax.ShapeDtypeStruct((16, D), F32),
            jax.ShapeDtypeStruct((SRC, ROWS, 2 * HD), BF16),
            jax.ShapeDtypeStruct((4, 16, 16, D), BF16),
        ),
        in_specs=[pl.BlockSpec(memory_space=pl.ANY)] * 3,
        out_specs=(pl.BlockSpec(memory_space=pl.ANY),) * 3,
        scratch_shapes=[
            vmem((SRC, TOK, D), BF16),
            vmem((SRC, TOK, TOPK * HD + 128), BF16),
            vmem((16, D), BF16),
            vmem((2, 4, 2, 16, D), BF16),
            vmem((OWN, ROWS, D), BF16),
            vmem((OWN, ROWS, HD), BF16),
            vmem((OWN, ROWS, 128), F32),
            vmem((TOPK * TOK, 2 * HD), BF16),
            vmem((OWN * MAIN, TOPK * TOK), BF16),
            vmem((OWN * MAIN, TOPK * TOK), BF16),
            vmem((OWN * MAIN, SRC * TOK), BF16),
            vmem((OWN * MAIN, 2 * HD), F32),
            vmem((OWN, 4, 32, D), BF16),
            vmem((OWN, 2, 32, HALF), BF16),
            vmem((OWN, 2, 32, D), BF16),
            vmem((OWN, 2, 32, HALF), BF16),
            vmem((FAR, 16, D), F32),
            vmem((FAR - 1, 16, D), F32),
            vmem((2 * OWN, 16, D), F32),
            vmem((SRC, ROWS, 2 * HD), BF16),
            vmem((OWN * MAIN, 2 * HD), BF16),
            sems((2,)),
            sems((8, 2)),
            sems((8, 2)),
            sems((2,)),
            sems,
            sems((2, FAR)),
            sems((2, FAR)),
            sems((2, 16)),
            sems((2, 16)),
            sems((2, 16)),
            sems((2, 16)),
            sems((4,)),
            sems((4,)),
            sems((2, FAR)),
            sems((2, FAR)),
            sems((2,)),
            sems((OWN, 4)),
            sems((OWN, 4)),
            sems((OWN, 2)),
            sems((OWN, 2)),
            sems((2 * OWN,)),
            sems((FAR,)),
            sems((FAR - 1,)),
            sems,
            sems((SRC,)),
            sems((SRC,)),
            sems,
        ],
        compiler_params=pltpu.CompilerParams(
            collective_id=0, has_side_effects=True, vmem_limit_bytes=67043328
        ),
    )(grads, small, proj)


def return_kernel(routes_ref, back_ref, head_ref, gate_ref):
    routes = routes_ref[...]
    experts = lax.broadcasted_iota(jnp.int32, (TOK, 128), 1)
    named = [(routes[:, k : k + 1] == experts).astype(F32) for k in range(TOPK)]
    chosen = functools.reduce(lambda a, b: a + b, named)
    lower = (iota((TOK, TOK), 1) < iota((TOK, TOK), 0)).astype(BF16)
    before = jnp.dot(lower, chosen.astype(BF16), preferred_element_type=F32)
    rows = lax.broadcasted_iota(jnp.int32, (TOK, SRC * ROWS), 1)
    gates = jnp.zeros((TOK, 128), F32)
    for k in range(TOPK):
        expert = routes[:, k : k + 1]
        slot = jnp.sum(named[k] * before, axis=1, keepdims=True).astype(jnp.int32)
        owner = 2 * (expert >> 4) + (expert & 1)
        index = (expert & 15) >> 1
        place = jnp.where(
            slot < MAIN, index * MAIN + slot, OWN * MAIN + OVER * index + slot - MAIN
        )
        pick = (rows == owner * ROWS + place).astype(F32).astype(BF16)
        block = jnp.dot(pick, back_ref[...], preferred_element_type=F32)
        head_ref[:, k * HD : (k + 1) * HD] = block[:, 0:HD].astype(BF16)
        gates = jnp.where(experts == k, block[:, HD:], gates)
    gate_ref[...] = gates[:, 0:TOPK].astype(BF16)


def put_back(routes, back):
    return pl.pallas_call(
        return_kernel,
        out_shape=(
            jax.ShapeDtypeStruct((TOK, TOPK * HD), BF16),
            jax.ShapeDtypeStruct((TOK, TOPK), BF16),
        ),
        compiler_params=pltpu.CompilerParams(vmem_limit_bytes=32 << 20),
    )(routes, back)


def local(head_outputs, out_grad, gate_weights, route_ids, out_proj):
    small = jnp.concatenate(
        [
            head_outputs.reshape(TOK, TOPK * HD),
            gate_weights,
            route_ids.astype(BF16),
            jnp.zeros((TOK, 128 - 2 * TOPK), BF16),
        ],
        axis=1,
    )
    grad_proj, got, _ = owner_work(out_grad, small, out_proj[0])
    grad_head, grad_gate = put_back(route_ids, got.reshape(SRC * ROWS, 2 * HD))
    return grad_head.reshape(TOK, TOPK, HD), grad_gate, grad_proj[None]


def solution(mesh):
    return jax.shard_map(
        local,
        mesh=mesh,
        in_specs=(
            P(("dp", "expert"), None, None),
            P(("dp", "expert"), None),
            P(("dp", "expert"), None),
            P(("dp", "expert"), None),
            P("expert", None, None),
        ),
        out_specs=(
            P(("dp", "expert"), None, None),
            P(("dp", "expert"), None),
            P("expert", "dp", None),
        ),
        check_vma=False,
    )
```

```python
import functools

import jax
import jax.numpy as jnp
from jax import lax
from jax.experimental import pallas as pl
from jax.experimental.pallas import tpu as pltpu
from jax.sharding import PartitionSpec as P

CAP = 1.5
F32 = jnp.float32
BF16 = jnp.bfloat16

SRC = 8
OWN = 8
TOK = 128
TOPK = 8
HD = 128
D = 4096
MAIN = 16
OVER = 2
ROWS = SRC * (MAIN + OVER)
STEP = 512


def iota(shape, axis):
    return lax.broadcasted_iota(jnp.int32, shape, axis).astype(F32)


def dispatch_source(base, s, xg, xs, gx, gh, gg, hcat, qm, qo, po, over):
    upper = (iota((TOK, TOK), 0) < iota((TOK, TOK), 1)).astype(BF16)
    lane = iota((TOK, 128), 1)
    slot = iota((MAIN, TOK), 0)
    meta = xs[s, :, TOPK * HD :].astype(F32)
    routes = meta.T[TOPK : 2 * TOPK, :]
    named = [(routes == (base + 2 * j).astype(F32)).astype(F32) for j in range(OWN)]
    chosen = jnp.concatenate([jnp.sum(n, axis=0, keepdims=True) for n in named], axis=0)
    before = jnp.dot(chosen.astype(BF16), upper, preferred_element_type=F32)
    shift = (OVER * s - MAIN).astype(F32)
    columns = pl.ds(pl.multiple_of(s * TOK, TOK), TOK)
    picks = []
    for j in range(OWN):
        rows = slice(j * MAIN, (j + 1) * MAIN)
        pos = before[j : j + 1, :]
        spot = jnp.where(chosen[j : j + 1, :] > 0, pos, -1.0)
        picks.append((spot == slot).astype(F32))
        tardy = jnp.where(spot >= MAIN, spot + shift, -1.0)
        po[rows, columns] = (tardy == slot).astype(F32).astype(BF16)
        own = jnp.where(named[j] > 0, pos, -1.0)
        own_tardy = jnp.where(own >= MAIN, own + shift, -1.0)
        for k in range(TOPK):
            piece = slice(k * TOK, (k + 1) * TOK)
            qm[rows, piece] = (own[k : k + 1, :] == slot).astype(F32).astype(BF16)
            qo[rows, piece] = (own_tardy[k : k + 1, :] == slot).astype(F32).astype(BF16)
    pick = jnp.concatenate(picks, axis=0).astype(BF16)
    for k in range(TOPK):
        piece = slice(k * TOK, (k + 1) * TOK)
        hcat[piece, 0:HD] = xs[s, :, k * HD : (k + 1) * HD]
        hcat[piece, HD : 2 * HD] = jnp.where(lane == k, meta, 0.0).astype(BF16)
    out_rows = pl.ds(pl.multiple_of(s * MAIN, MAIN), MAIN)
    for c in range(0, D, STEP):
        block = jnp.dot(pick, xg[s, :, c : c + STEP], preferred_element_type=F32)
        gx[:, out_rows, c : c + STEP] = block.astype(BF16).reshape(OWN, MAIN, STEP)
    block = jnp.dot(qm[...], hcat[...], preferred_element_type=F32)
    gh[:, out_rows, :] = block[:, 0:HD].astype(BF16).reshape(OWN, MAIN, HD)
    gate = jnp.sum(block[:, HD:], axis=1, keepdims=True)
    gg[:, out_rows, :] = jnp.broadcast_to(gate, (OWN * MAIN, 128)).reshape(OWN, MAIN, 128)
    over[...] += jnp.dot(qo[...], hcat[...], preferred_element_type=F32)


def dispatch_rest(xg, gx, gh, gg, po, over):
    tail = slice(SRC * MAIN, ROWS)
    width = 2 * 128
    for c in range(0, D, width):
        tokens = xg[:, :, c : c + width].reshape(SRC * TOK, width)
        block = jnp.dot(po[...], tokens, preferred_element_type=F32)
        gx[:, tail, c : c + width] = block.astype(BF16).reshape(OWN, SRC * OVER, width)
    gh[:, tail, :] = over[:, 0:HD].astype(BF16).reshape(OWN, SRC * OVER, HD)
    gate = jnp.sum(over[:, HD:], axis=1, keepdims=True)
    gg[:, tail, :] = jnp.broadcast_to(gate, (OWN * SRC * OVER, 128)).reshape(OWN, SRC * OVER, 128)


MESH = pl.DeviceIdType.MESH
HALF = D // 2
ZFIRST = 2816
FAR = 8


def place():
    dp, expert = lax.axis_index("dp"), lax.axis_index("expert")
    y, z = expert // 16, lax.rem(expert, 16)
    x, core = dp // 2, lax.rem(dp, 2)
    odd = lax.rem(z, 2)
    partner = (2 * y + odd, 16 * x + z - odd + core)
    alone = jnp.logical_and(x == y, core == odd)
    return dp, y, z, partner, alone


def meet(peers, partner, alone):
    barrier = pltpu.get_barrier_semaphore()
    for peer in peers:
        pl.semaphore_signal(barrier, inc=1, device_id=peer, device_id_type=MESH)

    @pl.when(jnp.logical_not(alone))
    def _():
        pl.semaphore_signal(barrier, inc=1, device_id=partner, device_id_type=MESH)

    pl.semaphore_wait(barrier, len(peers) + jnp.where(alone, 0, 1))


def send(src, dst, send_sem, recv_sem, device):
    return pltpu.make_async_remote_copy(
        src_ref=src,
        dst_ref=dst,
        send_sem=send_sem,
        recv_sem=recv_sem,
        device_id=device,
        device_id_type=MESH,
    )


def expert_step(i, j, wbuf, slot, gx, gh, gg, part, ret, late):
    heads = gh[j]
    gate = gg[j]
    head_grad = jnp.zeros((ROWS, HD), F32)
    gate_sum = jnp.zeros((ROWS, 128), F32)
    for c in range(0, D, STEP):
        weight = wbuf[slot, :, :, :, c : c + STEP].reshape(HD, STEP)
        pre = jnp.dot(heads, weight, preferred_element_type=F32)
        capped = jnp.tanh(pre * (1.0 / CAP))
        grad = gx[j, :, c : c + STEP].astype(F32)
        grad_capped = grad * capped
        rest = grad - grad_capped * capped
        parts = []
        for b in range(0, STEP, 128):
            gate_sum = gate_sum + grad_capped[:, b : b + 128]
            parts.append((gate * rest[:, b : b + 128]).astype(BF16))
        grad_pre = jnp.concatenate(parts, axis=1)
        head_grad = head_grad + lax.dot_general(
            grad_pre, weight, (((1,), (1,)), ((), ())), preferred_element_type=F32
        )
        grown = lax.dot_general(
            heads, grad_pre, (((0,), (0,)), ((), ())), preferred_element_type=F32
        )
        part[i, :, :, c : c + STEP] = grown.astype(BF16).reshape(4, 32, STEP)
    gate_grad = CAP * jnp.sum(gate_sum, axis=1, keepdims=True)
    both = jnp.concatenate([head_grad, jnp.broadcast_to(gate_grad, (ROWS, 128))], axis=1)
    both = both.astype(BF16)
    rows = pl.ds(pl.multiple_of(j * MAIN, MAIN), MAIN)
    ret[:, rows, :] = both[0 : SRC * MAIN].reshape(SRC, MAIN, 2 * HD)
    late[rows, :] = both[SRC * MAIN :]


def owner_kernel(
    grad_ref, small_ref, proj_ref, out_ref, got_ref, w_ref,
    xg, xs, own, wbuf, gx, gh, gg, hcat, qm, qo, po, over,
    part, a_in, b_in, comb, zl, zr, zout, zsum, ret, late,
    mine_sem, ts, tr, own_sem, hold_sem, hs, hr, ys, yr, fs, fr, es, er, bs, br,
    w_sem, ps, pr, cs, cr, zs, zlr, zrr, out_sem, rs, rr, keep_sem,
):
    dp, y, z, partner, alone = place()
    x, core = dp // 2, lax.rem(dp, 2)
    ring = lambda v, step, n: lax.rem(v + step + n, n)
    yu, yd, y2 = ring(y, 1, 4), ring(y, -1, 4), ring(y, 2, 4)
    up, down = (dp, yu * 16 + z), (dp, yd * 16 + z)
    right, left = (dp, y * 16 + ring(z, 1, 16)), (dp, y * 16 + ring(z, -1, 16))
    here = y * 16 + z
    others = [(lax.rem(dp + k, SRC), here) for k in range(1, SRC)]
    base = (dp // 2) * 16 + lax.rem(dp, 2)
    low, high = pl.ds(0, HALF), pl.ds(HALF, HALF)

    group = lambda step, flip: 2 * ring(x, step, 4) + (1 - core if flip else core)
    mine = (
        pltpu.make_async_copy(grad_ref, xg.at[dp], mine_sem.at[0]),
        pltpu.make_async_copy(small_ref, xs.at[dp], mine_sem.at[1]),
    )

    def tokens(n):
        device = (group((1, -1, 1, -1, 0, 0, 0, 0)[n], n >= 4), here)
        origin = group((0, 0, -1, 1, 0, -1, 1, 2)[n], False)
        whole = n in (0, 1, 4, 5, 6, 7)
        first = n in (0, 1, 4)
        wide = grad_ref if first else xg.at[origin]
        narrow = small_ref if first else xs.at[origin]
        to_wide, to_narrow = xg.at[origin], xs.at[origin]
        if not whole:
            half = low if n == 2 else high
            wide, to_wide = xg.at[origin, :, half], xg.at[origin, :, half]
        out = [send(wide, to_wide, ts.at[n, 0], tr.at[n, 0], device)]
        if n != 3:
            out.append(send(narrow, to_narrow, ts.at[n, 1], tr.at[n, 1], device))
        return out

    def start(copies):
        for one in copies:
            one.start()

    def arrive(copies):
        for one in copies:
            one.wait_recv()

    start(mine)
    meet([up, down, right, left] + others, partner, alone)

    slab = proj_ref.at[pl.ds(pl.multiple_of(dp * 16, 16), 16), :]
    trade = send(slab, own, own_sem.at[0], own_sem.at[1], partner)
    local = pltpu.make_async_copy(slab, own, own_sem.at[1])

    @pl.when(alone)
    def _():
        local.start()

    @pl.when(jnp.logical_not(alone))
    def _():
        trade.start()

    for n in (0, 1, 4):
        start(tokens(n))

    @pl.when(alone)
    def _():
        local.wait()

    @pl.when(jnp.logical_not(alone))
    def _():
        trade.wait()

    hold = pltpu.make_async_copy(own, w_ref.at[y, z], hold_sem)
    hold.start()

    zcols = pl.ds(0, ZFIRST)
    ycols = pl.ds(ZFIRST, D - ZFIRST)
    zhalf = (pl.ds(0, ZFIRST // 2), pl.ds(ZFIRST // 2, ZFIRST // 2))
    yhalf = (pl.ds(ZFIRST, (D - ZFIRST) // 2), pl.ds((D + ZFIRST) // 2, (D - ZFIRST) // 2))

    def along_z(src, col, way, hop):
        to = w_ref.at[y, col, :, zcols]
        return send(src, to, hs.at[way, hop], hr.at[way, hop], (right, left)[way])

    def along_y(src, col, way):
        to = w_ref.at[y, col, :, zcols]
        return send(src, to, ys.at[way, col], yr.at[way, col], (up, down)[way])

    def forward(row, col, way):
        block = w_ref.at[row, col, :, zhalf[way]]
        return send(block, block, fs.at[way, col], fr.at[way, col], (up, down)[way])

    def early_y(way):
        to = w_ref.at[y, z, :, ycols]
        return send(own.at[:, ycols], to, es.at[way], er.at[way], (up, down)[way])

    def early_forward(row, way):
        block = w_ref.at[row, z, :, yhalf[way]]
        return send(block, block, es.at[2 + way], er.at[2 + way], (up, down)[way])

    def bundle(col, way, hop):
        block = w_ref.at[:, col, :, ycols]
        return send(block, block, bs.at[way, hop], br.at[way, hop], (right, left)[way])

    mine_z = own.at[:, zcols]
    early_y(0).start()
    early_y(1).start()
    along_z(mine_z, z, 0, 0).start()
    along_z(mine_z, z, 1, 0).start()
    along_y(mine_z, z, 0).start()
    along_y(mine_z, z, 1).start()
    early_y(0).wait_recv()
    early_forward(yd, 0).start()
    early_y(1).wait_recv()
    early_forward(yu, 1).start()

    def column(step):
        away = (step + 1) // 2
        return lax.rem(z + 16 + jnp.where(lax.rem(step, 2) == 1, -away, away), 16)

    def pass_on(step):
        col = column(step)
        along_y(mine_z, col, 0).wait_recv()
        forward(yd, col, 0).start()
        along_y(mine_z, col, 1).wait_recv()
        forward(yu, col, 1).start()

    def settle(step, _):
        col = column(step)
        forward(y2, col, 0).wait_recv()
        forward(y2, col, 1).wait_recv()
        return 0

    def arrived_z(hop, way):
        col = ring(z, -hop if way == 0 else hop, 16)
        block = w_ref.at[y, col, :, zcols]
        along_z(block, col, way, hop - 1).wait_recv()

        @pl.when(hop < FAR - way)
        def _():
            along_z(block, col, way, hop).start()

        along_y(block, col, 0).start()
        along_y(block, col, 1).start()

    def arrived_bundle(hop, way):
        col = ring(z, -hop if way == 0 else hop, 16)
        bundle(col, way, hop - 1).wait_recv()

        @pl.when(hop < FAR - way)
        def _():
            bundle(col, way, hop).start()

    def expert_at(i):
        away = 4 - (i + 1) // 2
        return lax.rem(z // 2 + OWN + jnp.where(lax.rem(i, 2) == 1, away, -away), OWN)

    def weight_copy(i):
        slot = lax.rem(i, 2)
        pair = w_ref.at[:, pl.ds(2 * expert_at(i), 2)]
        return pltpu.make_async_copy(pair, wbuf.at[slot], w_sem.at[slot])

    over[...] = jnp.zeros_like(over)

    def gather_step(hop, _):
        @pl.when(hop <= FAR)
        def _():
            arrived_z(hop, 0)

        @pl.when(hop < FAR)
        def _():
            arrived_z(hop, 1)

        @pl.when(hop == 1)
        def _():
            early_forward(y2, 0).wait_recv()
            early_forward(y2, 1).wait_recv()
            hold.wait()
            bundle(z, 0, 0).start()
            bundle(z, 1, 0).start()

        @pl.when((hop >= 2) & (hop <= FAR + 1))
        def _():
            arrived_bundle(hop - 1, 0)

        @pl.when((hop >= 2) & (hop <= FAR))
        def _():
            arrived_bundle(hop - 1, 1)

        @pl.when(hop == 2)
        def _():
            pass_on(0)

        @pl.when(hop >= 3)
        def _():
            pass_on(2 * (hop - 2) - 1)

        @pl.when((hop >= 3) & (hop < FAR + 2))
        def _():
            pass_on(2 * (hop - 2))

        n = hop - 3

        @pl.when(n == 0)
        def _():
            for one in mine:
                one.wait()

        @pl.when(n == 1)
        def _():
            arrive(tokens(4))

        @pl.when(n == 2)
        def _():
            arrive(tokens(0))
            start(tokens(2))
            start(tokens(5))
            arrive(tokens(1))
            start(tokens(3))
            start(tokens(6))

        @pl.when(n == 4)
        def _():
            arrive(tokens(5))

        @pl.when(n == 5)
        def _():
            arrive(tokens(6))

        @pl.when(n == 6)
        def _():
            arrive(tokens(2))
            arrive(tokens(3))
            start(tokens(7))

        @pl.when(n == 7)
        def _():
            arrive(tokens(7))

        @pl.when(n >= 0)
        def _():
            step = jnp.where(n < 2, 0, jnp.where(n >= 6, 2, jnp.where(lax.rem(n, 2) == 0, -1, 1)))
            flip = (n == 1) | (n == 4) | (n == 5) | (n == 7)
            s = 2 * ring(x, step, 4) + jnp.where(flip, 1 - core, core)
            dispatch_source(base, s, xg, xs, gx, gh, gg, hcat, qm, qo, po, over)

        return 0

    with jax.named_scope("gather"):
        lax.fori_loop(1, FAR + 3, gather_step, 0)
    with jax.named_scope("rest"):
        dispatch_rest(xg, gx, gh, gg, po, over)
    with jax.named_scope("settle"):
        lax.fori_loop(0, 16, settle, 0)
    weight_copy(0).start()

    def first_sends(i):
        return (
            send(part.at[i, y2, :, low], a_in.at[i, 0], ps.at[i, 0], pr.at[i, 0], up),
            send(part.at[i, y2, :, high], a_in.at[i, 1], ps.at[i, 1], pr.at[i, 1], down),
            send(part.at[i, yu, :, high], b_in.at[i, 0, :, high], ps.at[i, 2], pr.at[i, 2], up),
            send(part.at[i, yd, :, low], b_in.at[i, 1, :, low], ps.at[i, 3], pr.at[i, 3], down),
        )

    def second_sends(i):
        return (
            send(comb.at[i, 0], b_in.at[i, 0, :, low], cs.at[i, 0], cr.at[i, 0], up),
            send(comb.at[i, 1], b_in.at[i, 1, :, high], cs.at[i, 1], cr.at[i, 1], down),
        )

    def combine(i):
        first, second = first_sends(i), second_sends(i)
        first[0].wait_recv()
        comb[i, 0] = (part[i, yu, :, low].astype(F32) + a_in[i, 0].astype(F32)).astype(BF16)
        second[0].start()
        first[1].wait_recv()
        comb[i, 1] = (part[i, yd, :, high].astype(F32) + a_in[i, 1].astype(F32)).astype(BF16)
        second[1].start()

    def to_right(k, slot):
        return send(zout.at[k], zl.at[slot], zs.at[k], zlr.at[slot], right)

    def to_left(k, slot):
        return send(zout.at[k], zr.at[slot], zs.at[k], zrr.at[slot], left)

    def to_partner(k):
        return send(zsum.at[k], out_ref, zs.at[k], out_sem, partner)

    def to_self(k):
        return pltpu.make_async_copy(zsum.at[k], out_ref, zs.at[k])

    def finish(i):
        for one in first_sends(i)[2:] + second_sends(i):
            one.wait_recv()
        total = (
            part[i, y].astype(F32) + b_in[i, 0].astype(F32) + b_in[i, 1].astype(F32)
        )
        for c in range(2):
            zsum[2 * i + c] = total[16 * c : 16 * (c + 1)]

    def along(i, lagging):
        j = expert_at(i)
        for c in range(2):
            k = 2 * i + c
            ahead = lax.rem(2 * j + c - z + 16, 16)
            behind = lax.rem(16 - ahead, 16)
            odd = lax.rem(z, 2) == 1
            lag = jnp.where(ahead <= FAR, odd, jnp.logical_not(odd)) | (ahead == 0)
            now = lag if lagging else jnp.logical_not(lag)

            @pl.when(now & (ahead < FAR))
            def _():
                to_right(k, ahead).wait_recv()
                zsum[k] += zl[ahead].astype(F32)

            @pl.when(now & (behind < FAR - 1))
            def _():
                to_left(k, behind).wait_recv()
                zsum[k] += zr[behind].astype(F32)

            @pl.when(now & (ahead >= 1) & (ahead <= FAR))
            def _():
                zout[k] = zsum[k].astype(BF16)
                to_right(k, ahead - 1).start()

            @pl.when(now & (ahead > FAR))
            def _():
                zout[k] = zsum[k].astype(BF16)
                to_left(k, behind - 1).start()

            @pl.when(now & (ahead == 0) & alone)
            def _():
                to_self(k).start()

            @pl.when(now & (ahead == 0) & jnp.logical_not(alone))
            def _():
                to_partner(k).start()

    def returns():
        out = []
        for k in range(1, SRC):
            to = lax.rem(dp + k, SRC)
            out.append(send(ret.at[to], got_ref.at[dp], rs.at[k], rr.at[k], others[k - 1]))
        return out

    keep = pltpu.make_async_copy(ret.at[dp], got_ref.at[dp], keep_sem)

    def one_expert(i, _):
        @pl.when(i < OWN)
        def _():
            @pl.when(i + 1 < OWN)
            def _():
                weight_copy(i + 1).start()

            weight_copy(i).wait()
            with jax.named_scope("expert"):
                expert_step(i, expert_at(i), wbuf, lax.rem(i, 2), gx, gh, gg, part, ret, late)
            for one in first_sends(i):
                one.start()

        @pl.when(i == OWN - 1)
        def _():
            to = lax.broadcasted_iota(jnp.int32, (OWN * MAIN, OWN * MAIN), 0)
            source = lax.broadcasted_iota(jnp.int32, (OWN * MAIN, OWN * MAIN), 1)
            want = (lax.rem(to, 16) // 2) * 16 + (to // 16) * 2 + lax.rem(to, 2)
            shuffle = (source == want).astype(F32).astype(BF16)
            moved = jnp.dot(shuffle, late[...], preferred_element_type=F32).astype(BF16)
            ret[:, OWN * MAIN :, :] = moved.reshape(SRC, OWN * OVER, 2 * HD)
            for one in returns():
                one.start()
            keep.start()

        @pl.when(jnp.logical_and(i >= 1, i <= OWN))
        def _():
            with jax.named_scope("combine"):
                combine(i - 1)

        @pl.when(jnp.logical_and(i >= 2, i <= OWN + 1))
        def _():
            with jax.named_scope("finish"):
                finish(i - 2)
            with jax.named_scope("along"):
                along(i - 2, False)

        @pl.when(i >= 3)
        def _():
            with jax.named_scope("lagging"):
                along(i - 3, True)

        return 0

    lax.fori_loop(0, OWN + 3, one_expert, 0)
    with jax.named_scope("returned"):
        for one in returns():
            one.wait()
        keep.wait()

    @pl.when(jnp.logical_not(alone))
    def _():
        to_partner(0).wait_recv()

    def drain(i, _):
        for one in first_sends(i) + second_sends(i):
            one.wait_send()
        for c in range(2):
            k = 2 * i + c
            last = (i == OWN - 1) & (lax.rem(z, 2) == c)

            @pl.when(jnp.logical_not(last))
            def _():
                to_right(k, 0).wait_send()

            @pl.when(last & alone)
            def _():
                to_self(k).wait()

            @pl.when(last & jnp.logical_not(alone))
            def _():
                to_partner(k).wait_send()

        return 0

    lax.fori_loop(0, OWN, drain, 0)
    for n in range(8):
        for one in tokens(n):
            one.wait_send()
    for hop in range(FAR):
        for way in range(2):
            if hop < FAR - way:
                along_z(mine_z, z, way, hop).wait_send()
                bundle(z, way, hop).wait_send()
    for way in range(2):
        early_y(way).wait_send()
        early_forward(y2, way).wait_send()

    def drain_y(col, _):
        for way in range(2):
            along_y(mine_z, col, way).wait_send()
            forward(y2, col, way).wait_send()
        return 0

    lax.fori_loop(0, 16, drain_y, 0)


def owner_work(grads, small, proj):
    sems = pltpu.SemaphoreType.DMA
    vmem = pltpu.VMEM
    return pl.pallas_call(
        owner_kernel,
        out_shape=(
            jax.ShapeDtypeStruct((16, D), F32),
            jax.ShapeDtypeStruct((SRC, ROWS, 2 * HD), BF16),
            jax.ShapeDtypeStruct((4, 16, 16, D), BF16),
        ),
        in_specs=[pl.BlockSpec(memory_space=pl.ANY)] * 3,
        out_specs=(pl.BlockSpec(memory_space=pl.ANY),) * 3,
        scratch_shapes=[
            vmem((SRC, TOK, D), BF16),
            vmem((SRC, TOK, TOPK * HD + 128), BF16),
            vmem((16, D), BF16),
            vmem((2, 4, 2, 16, D), BF16),
            vmem((OWN, ROWS, D), BF16),
            vmem((OWN, ROWS, HD), BF16),
            vmem((OWN, ROWS, 128), F32),
            vmem((TOPK * TOK, 2 * HD), BF16),
            vmem((OWN * MAIN, TOPK * TOK), BF16),
            vmem((OWN * MAIN, TOPK * TOK), BF16),
            vmem((OWN * MAIN, SRC * TOK), BF16),
            vmem((OWN * MAIN, 2 * HD), F32),
            vmem((OWN, 4, 32, D), BF16),
            vmem((OWN, 2, 32, HALF), BF16),
            vmem((OWN, 2, 32, D), BF16),
            vmem((OWN, 2, 32, HALF), BF16),
            vmem((FAR, 16, D), BF16),
            vmem((FAR - 1, 16, D), BF16),
            vmem((2 * OWN, 16, D), BF16),
            vmem((2 * OWN, 16, D), F32),
            vmem((SRC, ROWS, 2 * HD), BF16),
            vmem((OWN * MAIN, 2 * HD), BF16),
            sems((2,)),
            sems((8, 2)),
            sems((8, 2)),
            sems((2,)),
            sems,
            sems((2, FAR)),
            sems((2, FAR)),
            sems((2, 16)),
            sems((2, 16)),
            sems((2, 16)),
            sems((2, 16)),
            sems((4,)),
            sems((4,)),
            sems((2, FAR)),
            sems((2, FAR)),
            sems((2,)),
            sems((OWN, 4)),
            sems((OWN, 4)),
            sems((OWN, 2)),
            sems((OWN, 2)),
            sems((2 * OWN,)),
            sems((FAR,)),
            sems((FAR - 1,)),
            sems,
            sems((SRC,)),
            sems((SRC,)),
            sems,
        ],
        compiler_params=pltpu.CompilerParams(
            collective_id=0, has_side_effects=True, vmem_limit_bytes=67043328
        ),
    )(grads, small, proj)


def return_kernel(routes_ref, back_ref, head_ref, gate_ref):
    routes = routes_ref[...]
    experts = lax.broadcasted_iota(jnp.int32, (TOK, 128), 1)
    named = [(routes[:, k : k + 1] == experts).astype(F32) for k in range(TOPK)]
    chosen = functools.reduce(lambda a, b: a + b, named)
    lower = (iota((TOK, TOK), 1) < iota((TOK, TOK), 0)).astype(BF16)
    before = jnp.dot(lower, chosen.astype(BF16), preferred_element_type=F32)
    rows = lax.broadcasted_iota(jnp.int32, (TOK, SRC * ROWS), 1)
    gates = jnp.zeros((TOK, 128), F32)
    for k in range(TOPK):
        expert = routes[:, k : k + 1]
        slot = jnp.sum(named[k] * before, axis=1, keepdims=True).astype(jnp.int32)
        owner = 2 * (expert >> 4) + (expert & 1)
        index = (expert & 15) >> 1
        place = jnp.where(
            slot < MAIN, index * MAIN + slot, OWN * MAIN + OVER * index + slot - MAIN
        )
        pick = (rows == owner * ROWS + place).astype(F32).astype(BF16)
        block = jnp.dot(pick, back_ref[...], preferred_element_type=F32)
        head_ref[:, k * HD : (k + 1) * HD] = block[:, 0:HD].astype(BF16)
        gates = jnp.where(experts == k, block[:, HD:], gates)
    gate_ref[...] = gates[:, 0:TOPK].astype(BF16)


def put_back(routes, back):
    return pl.pallas_call(
        return_kernel,
        out_shape=(
            jax.ShapeDtypeStruct((TOK, TOPK * HD), BF16),
            jax.ShapeDtypeStruct((TOK, TOPK), BF16),
        ),
        compiler_params=pltpu.CompilerParams(vmem_limit_bytes=32 << 20),
    )(routes, back)


def local(head_outputs, out_grad, gate_weights, route_ids, out_proj):
    small = jnp.concatenate(
        [
            head_outputs.reshape(TOK, TOPK * HD),
            gate_weights,
            route_ids.astype(BF16),
            jnp.zeros((TOK, 128 - 2 * TOPK), BF16),
        ],
        axis=1,
    )
    grad_proj, got, _ = owner_work(out_grad, small, out_proj[0])
    grad_head, grad_gate = put_back(route_ids, got.reshape(SRC * ROWS, 2 * HD))
    return grad_head.reshape(TOK, TOPK, HD), grad_gate, grad_proj[None]


def solution(mesh):
    return jax.shard_map(
        local,
        mesh=mesh,
        in_specs=(
            P(("dp", "expert"), None, None),
            P(("dp", "expert"), None),
            P(("dp", "expert"), None),
            P(("dp", "expert"), None),
            P("expert", None, None),
        ),
        out_specs=(
            P(("dp", "expert"), None, None),
            P(("dp", "expert"), None),
            P("expert", "dp", None),
        ),
        check_vma=False,
    )
```

```python
import functools

import jax
import jax.numpy as jnp
from jax import lax
from jax.experimental import pallas as pl
from jax.experimental.pallas import tpu as pltpu
from jax.sharding import PartitionSpec as P

CAP = 1.5
F32 = jnp.float32
BF16 = jnp.bfloat16

SRC = 8
OWN = 8
TOK = 128
TOPK = 8
HD = 128
D = 4096
MAIN = 16
OVER = 2
ROWS = SRC * (MAIN + OVER)
STEP = 512


def iota(shape, axis):
    return lax.broadcasted_iota(jnp.int32, shape, axis).astype(F32)


def dispatch_source(base, s, xg, xs, gx, gh, gg, hcat, qm, qo, po, over):
    upper = (iota((TOK, TOK), 0) < iota((TOK, TOK), 1)).astype(BF16)
    lane = iota((TOK, 128), 1)
    slot = iota((MAIN, TOK), 0)
    meta = xs[s, :, TOPK * HD :].astype(F32)
    routes = meta.T[TOPK : 2 * TOPK, :]
    named = [(routes == (base + 2 * j).astype(F32)).astype(F32) for j in range(OWN)]
    chosen = jnp.concatenate([jnp.sum(n, axis=0, keepdims=True) for n in named], axis=0)
    before = jnp.dot(chosen.astype(BF16), upper, preferred_element_type=F32)
    shift = (OVER * s - MAIN).astype(F32)
    columns = pl.ds(pl.multiple_of(s * TOK, TOK), TOK)
    picks = []
    for j in range(OWN):
        rows = slice(j * MAIN, (j + 1) * MAIN)
        pos = before[j : j + 1, :]
        spot = jnp.where(chosen[j : j + 1, :] > 0, pos, -1.0)
        picks.append((spot == slot).astype(F32))
        tardy = jnp.where(spot >= MAIN, spot + shift, -1.0)
        po[rows, columns] = (tardy == slot).astype(F32).astype(BF16)
        own = jnp.where(named[j] > 0, pos, -1.0)
        own_tardy = jnp.where(own >= MAIN, own + shift, -1.0)
        for k in range(TOPK):
            piece = slice(k * TOK, (k + 1) * TOK)
            qm[rows, piece] = (own[k : k + 1, :] == slot).astype(F32).astype(BF16)
            qo[rows, piece] = (own_tardy[k : k + 1, :] == slot).astype(F32).astype(BF16)
    pick = jnp.concatenate(picks, axis=0).astype(BF16)
    for k in range(TOPK):
        piece = slice(k * TOK, (k + 1) * TOK)
        hcat[piece, 0:HD] = xs[s, :, k * HD : (k + 1) * HD]
        hcat[piece, HD : 2 * HD] = jnp.where(lane == k, meta, 0.0).astype(BF16)
    out_rows = pl.ds(pl.multiple_of(s * MAIN, MAIN), MAIN)
    for c in range(0, D, STEP):
        block = jnp.dot(pick, xg[s, :, c : c + STEP], preferred_element_type=F32)
        gx[:, out_rows, c : c + STEP] = block.astype(BF16).reshape(OWN, MAIN, STEP)
    block = jnp.dot(qm[...], hcat[...], preferred_element_type=F32)
    gh[:, out_rows, :] = block[:, 0:HD].astype(BF16).reshape(OWN, MAIN, HD)
    gate = jnp.sum(block[:, HD:], axis=1, keepdims=True)
    gg[:, out_rows, :] = jnp.broadcast_to(gate, (OWN * MAIN, 128)).reshape(OWN, MAIN, 128)
    over[...] += jnp.dot(qo[...], hcat[...], preferred_element_type=F32)


def dispatch_rest(xg, gx, gh, gg, po, over):
    tail = slice(SRC * MAIN, ROWS)
    width = 2 * 128
    for c in range(0, D, width):
        tokens = xg[:, :, c : c + width].reshape(SRC * TOK, width)
        block = jnp.dot(po[...], tokens, preferred_element_type=F32)
        gx[:, tail, c : c + width] = block.astype(BF16).reshape(OWN, SRC * OVER, width)
    gh[:, tail, :] = over[:, 0:HD].astype(BF16).reshape(OWN, SRC * OVER, HD)
    gate = jnp.sum(over[:, HD:], axis=1, keepdims=True)
    gg[:, tail, :] = jnp.broadcast_to(gate, (OWN * SRC * OVER, 128)).reshape(OWN, SRC * OVER, 128)


MESH = pl.DeviceIdType.MESH
HALF = D // 2
ZFIRST = 3584
FAR = 8


def place():
    dp, expert = lax.axis_index("dp"), lax.axis_index("expert")
    y, z = expert // 16, lax.rem(expert, 16)
    x, core = dp // 2, lax.rem(dp, 2)
    odd = lax.rem(z, 2)
    partner = (2 * y + odd, 16 * x + z - odd + core)
    alone = jnp.logical_and(x == y, core == odd)
    return dp, y, z, partner, alone


def meet(peers, partner, alone):
    barrier = pltpu.get_barrier_semaphore()
    for peer in peers:
        pl.semaphore_signal(barrier, inc=1, device_id=peer, device_id_type=MESH)

    @pl.when(jnp.logical_not(alone))
    def _():
        pl.semaphore_signal(barrier, inc=1, device_id=partner, device_id_type=MESH)

    pl.semaphore_wait(barrier, len(peers) + jnp.where(alone, 0, 1))


def send(src, dst, send_sem, recv_sem, device):
    return pltpu.make_async_remote_copy(
        src_ref=src,
        dst_ref=dst,
        send_sem=send_sem,
        recv_sem=recv_sem,
        device_id=device,
        device_id_type=MESH,
    )


def expert_step(i, j, wbuf, slot, gx, gh, gg, part, ret, late):
    heads = gh[j]
    gate = gg[j]
    head_grad = jnp.zeros((ROWS, HD), F32)
    gate_sum = jnp.zeros((ROWS, 128), F32)
    for c in range(0, D, STEP):
        weight = wbuf[slot, :, :, :, c : c + STEP].reshape(HD, STEP)
        pre = jnp.dot(heads, weight, preferred_element_type=F32)
        capped = jnp.tanh(pre * (1.0 / CAP))
        grad = gx[j, :, c : c + STEP].astype(F32)
        grad_capped = grad * capped
        rest = grad - grad_capped * capped
        parts = []
        for b in range(0, STEP, 128):
            gate_sum = gate_sum + grad_capped[:, b : b + 128]
            parts.append((gate * rest[:, b : b + 128]).astype(BF16))
        grad_pre = jnp.concatenate(parts, axis=1)
        head_grad = head_grad + lax.dot_general(
            grad_pre, weight, (((1,), (1,)), ((), ())), preferred_element_type=F32
        )
        grown = lax.dot_general(
            heads, grad_pre, (((0,), (0,)), ((), ())), preferred_element_type=F32
        )
        part[i, :, :, c : c + STEP] = grown.astype(BF16).reshape(4, 32, STEP)
    gate_grad = CAP * jnp.sum(gate_sum, axis=1, keepdims=True)
    both = jnp.concatenate([head_grad, jnp.broadcast_to(gate_grad, (ROWS, 128))], axis=1)
    both = both.astype(BF16)
    rows = pl.ds(pl.multiple_of(j * MAIN, MAIN), MAIN)
    ret[:, rows, :] = both[0 : SRC * MAIN].reshape(SRC, MAIN, 2 * HD)
    late[rows, :] = both[SRC * MAIN :]


def owner_kernel(
    grad_ref, small_ref, proj_ref, out_ref, got_ref, w_ref,
    xg, xs, own, wbuf, gx, gh, gg, hcat, qm, qo, po, over,
    part, a_in, b_in, comb, zl, zr, zout, zsum, ret, late,
    mine_sem, ts, tr, own_sem, hold_sem, hs, hr, ys, yr, fs, fr, es, er, bs, br,
    w_sem, ps, pr, cs, cr, zs, zlr, zrr, out_sem, rs, rr, keep_sem,
):
    dp, y, z, partner, alone = place()
    x, core = dp // 2, lax.rem(dp, 2)
    ring = lambda v, step, n: lax.rem(v + step + n, n)
    yu, yd, y2 = ring(y, 1, 4), ring(y, -1, 4), ring(y, 2, 4)
    up, down = (dp, yu * 16 + z), (dp, yd * 16 + z)
    right, left = (dp, y * 16 + ring(z, 1, 16)), (dp, y * 16 + ring(z, -1, 16))
    here = y * 16 + z
    others = [(lax.rem(dp + k, SRC), here) for k in range(1, SRC)]
    base = (dp // 2) * 16 + lax.rem(dp, 2)
    low, high = pl.ds(0, HALF), pl.ds(HALF, HALF)

    group = lambda step, flip: 2 * ring(x, step, 4) + (1 - core if flip else core)
    mine = (
        pltpu.make_async_copy(grad_ref, xg.at[dp], mine_sem.at[0]),
        pltpu.make_async_copy(small_ref, xs.at[dp], mine_sem.at[1]),
    )

    def tokens(n):
        device = (group((1, -1, 1, -1, 0, 0, 0, 0)[n], n >= 4), here)
        origin = group((0, 0, -1, 1, 0, -1, 1, 2)[n], False)
        whole = n in (0, 1, 4, 5, 6, 7)
        first = n in (0, 1, 4)
        wide = grad_ref if first else xg.at[origin]
        narrow = small_ref if first else xs.at[origin]
        to_wide, to_narrow = xg.at[origin], xs.at[origin]
        if not whole:
            half = low if n == 2 else high
            wide, to_wide = xg.at[origin, :, half], xg.at[origin, :, half]
        out = [send(wide, to_wide, ts.at[n, 0], tr.at[n, 0], device)]
        if n != 3:
            out.append(send(narrow, to_narrow, ts.at[n, 1], tr.at[n, 1], device))
        return out

    def start(copies):
        for one in copies:
            one.start()

    def arrive(copies):
        for one in copies:
            one.wait_recv()

    start(mine)
    meet([up, down, right, left] + others, partner, alone)

    slab = proj_ref.at[pl.ds(pl.multiple_of(dp * 16, 16), 16), :]
    trade = send(slab, own, own_sem.at[0], own_sem.at[1], partner)
    local = pltpu.make_async_copy(slab, own, own_sem.at[1])

    @pl.when(alone)
    def _():
        local.start()

    @pl.when(jnp.logical_not(alone))
    def _():
        trade.start()

    for n in (0, 1, 4):
        start(tokens(n))

    @pl.when(alone)
    def _():
        local.wait()

    @pl.when(jnp.logical_not(alone))
    def _():
        trade.wait()

    hold = pltpu.make_async_copy(own, w_ref.at[y, z], hold_sem)
    hold.start()

    zcols = pl.ds(0, ZFIRST)
    ycols = pl.ds(ZFIRST, D - ZFIRST)
    zhalf = (pl.ds(0, ZFIRST // 2), pl.ds(ZFIRST // 2, ZFIRST // 2))
    yhalf = (pl.ds(ZFIRST, (D - ZFIRST) // 2), pl.ds((D + ZFIRST) // 2, (D - ZFIRST) // 2))

    def along_z(src, col, way, hop):
        to = w_ref.at[y, col, :, zcols]
        return send(src, to, hs.at[way, hop], hr.at[way, hop], (right, left)[way])

    def along_y(src, col, way):
        to = w_ref.at[y, col, :, zcols]
        return send(src, to, ys.at[way, col], yr.at[way, col], (up, down)[way])

    def forward(row, col, way):
        block = w_ref.at[row, col, :, zhalf[way]]
        return send(block, block, fs.at[way, col], fr.at[way, col], (up, down)[way])

    def early_y(way):
        to = w_ref.at[y, z, :, ycols]
        return send(own.at[:, ycols], to, es.at[way], er.at[way], (up, down)[way])

    def early_forward(row, way):
        block = w_ref.at[row, z, :, yhalf[way]]
        return send(block, block, es.at[2 + way], er.at[2 + way], (up, down)[way])

    def bundle(col, way, hop):
        block = w_ref.at[:, col, :, ycols]
        return send(block, block, bs.at[way, hop], br.at[way, hop], (right, left)[way])

    mine_z = own.at[:, zcols]
    early_y(0).start()
    early_y(1).start()
    along_z(mine_z, z, 0, 0).start()
    along_z(mine_z, z, 1, 0).start()
    along_y(mine_z, z, 0).start()
    along_y(mine_z, z, 1).start()
    early_y(0).wait_recv()
    early_forward(yd, 0).start()
    early_y(1).wait_recv()
    early_forward(yu, 1).start()

    def column(step):
        away = (step + 1) // 2
        return lax.rem(z + 16 + jnp.where(lax.rem(step, 2) == 1, -away, away), 16)

    def pass_on(step):
        col = column(step)
        along_y(mine_z, col, 0).wait_recv()
        forward(yd, col, 0).start()
        along_y(mine_z, col, 1).wait_recv()
        forward(yu, col, 1).start()

    def settle(step, _):
        col = column(step)
        forward(y2, col, 0).wait_recv()
        forward(y2, col, 1).wait_recv()
        return 0

    def arrived_z(hop, way):
        col = ring(z, -hop if way == 0 else hop, 16)
        block = w_ref.at[y, col, :, zcols]
        along_z(block, col, way, hop - 1).wait_recv()

        @pl.when(hop < FAR - way)
        def _():
            along_z(block, col, way, hop).start()

        along_y(block, col, 0).start()
        along_y(block, col, 1).start()

    def arrived_bundle(hop, way):
        col = ring(z, -hop if way == 0 else hop, 16)
        bundle(col, way, hop - 1).wait_recv()

        @pl.when(hop < FAR - way)
        def _():
            bundle(col, way, hop).start()

    def expert_at(i):
        away = 4 - (i + 1) // 2
        return lax.rem(z // 2 + OWN + jnp.where(lax.rem(i, 2) == 1, away, -away), OWN)

    def weight_copy(i):
        slot = lax.rem(i, 2)
        pair = w_ref.at[:, pl.ds(2 * expert_at(i), 2)]
        return pltpu.make_async_copy(pair, wbuf.at[slot], w_sem.at[slot])

    over[...] = jnp.zeros_like(over)

    def gather_step(hop, _):
        @pl.when(hop <= FAR)
        def _():
            arrived_z(hop, 0)

        @pl.when(hop < FAR)
        def _():
            arrived_z(hop, 1)

        @pl.when(hop == 1)
        def _():
            early_forward(y2, 0).wait_recv()
            early_forward(y2, 1).wait_recv()
            hold.wait()
            bundle(z, 0, 0).start()
            bundle(z, 1, 0).start()

        @pl.when((hop >= 2) & (hop <= FAR + 1))
        def _():
            arrived_bundle(hop - 1, 0)

        @pl.when((hop >= 2) & (hop <= FAR))
        def _():
            arrived_bundle(hop - 1, 1)

        @pl.when(hop == 2)
        def _():
            pass_on(0)

        @pl.when(hop >= 3)
        def _():
            pass_on(2 * (hop - 2) - 1)

        @pl.when((hop >= 3) & (hop < FAR + 2))
        def _():
            pass_on(2 * (hop - 2))

        n = hop - 3

        @pl.when(n == 0)
        def _():
            for one in mine:
                one.wait()

        @pl.when(n == 1)
        def _():
            arrive(tokens(4))

        @pl.when(n == 2)
        def _():
            arrive(tokens(0))
            start(tokens(2))
            start(tokens(5))
            arrive(tokens(1))
            start(tokens(3))
            start(tokens(6))

        @pl.when(n == 4)
        def _():
            arrive(tokens(5))

        @pl.when(n == 5)
        def _():
            arrive(tokens(6))

        @pl.when(n == 6)
        def _():
            arrive(tokens(2))
            arrive(tokens(3))
            start(tokens(7))

        @pl.when(n == 7)
        def _():
            arrive(tokens(7))

        @pl.when(n >= 0)
        def _():
            step = jnp.where(n < 2, 0, jnp.where(n >= 6, 2, jnp.where(lax.rem(n, 2) == 0, -1, 1)))
            flip = (n == 1) | (n == 4) | (n == 5) | (n == 7)
            s = 2 * ring(x, step, 4) + jnp.where(flip, 1 - core, core)
            dispatch_source(base, s, xg, xs, gx, gh, gg, hcat, qm, qo, po, over)

        return 0

    with jax.named_scope("gather"):
        lax.fori_loop(1, FAR + 3, gather_step, 0)
    with jax.named_scope("rest"):
        dispatch_rest(xg, gx, gh, gg, po, over)
    with jax.named_scope("settle"):
        lax.fori_loop(0, 16, settle, 0)
    weight_copy(0).start()

    def first_sends(i):
        return (
            send(part.at[i, y2, :, low], a_in.at[i, 0], ps.at[i, 0], pr.at[i, 0], up),
            send(part.at[i, y2, :, high], a_in.at[i, 1], ps.at[i, 1], pr.at[i, 1], down),
            send(part.at[i, yu, :, high], b_in.at[i, 0, :, high], ps.at[i, 2], pr.at[i, 2], up),
            send(part.at[i, yd, :, low], b_in.at[i, 1, :, low], ps.at[i, 3], pr.at[i, 3], down),
        )

    def second_sends(i):
        return (
            send(comb.at[i, 0], b_in.at[i, 0, :, low], cs.at[i, 0], cr.at[i, 0], up),
            send(comb.at[i, 1], b_in.at[i, 1, :, high], cs.at[i, 1], cr.at[i, 1], down),
        )

    def combine(i):
        first, second = first_sends(i), second_sends(i)
        first[0].wait_recv()
        comb[i, 0] = (part[i, yu, :, low].astype(F32) + a_in[i, 0].astype(F32)).astype(BF16)
        second[0].start()
        first[1].wait_recv()
        comb[i, 1] = (part[i, yd, :, high].astype(F32) + a_in[i, 1].astype(F32)).astype(BF16)
        second[1].start()

    def to_right(k, slot):
        return send(zout.at[k], zl.at[slot], zs.at[k], zlr.at[slot], right)

    def to_left(k, slot):
        return send(zout.at[k], zr.at[slot], zs.at[k], zrr.at[slot], left)

    def to_partner(k):
        return send(zsum.at[k], out_ref, zs.at[k], out_sem, partner)

    def to_self(k):
        return pltpu.make_async_copy(zsum.at[k], out_ref, zs.at[k])

    def finish(i):
        for one in first_sends(i)[2:] + second_sends(i):
            one.wait_recv()
        total = (
            part[i, y].astype(F32) + b_in[i, 0].astype(F32) + b_in[i, 1].astype(F32)
        )
        for c in range(2):
            zsum[2 * i + c] = total[16 * c : 16 * (c + 1)]

    def along(i, lagging):
        j = expert_at(i)
        for c in range(2):
            k = 2 * i + c
            ahead = lax.rem(2 * j + c - z + 16, 16)
            behind = lax.rem(16 - ahead, 16)
            odd = lax.rem(z, 2) == 1
            lag = jnp.where(ahead <= FAR, odd, jnp.logical_not(odd)) | (ahead == 0)
            now = lag if lagging else jnp.logical_not(lag)

            @pl.when(now & (ahead < FAR))
            def _():
                to_right(k, ahead).wait_recv()
                zsum[k] += zl[ahead].astype(F32)

            @pl.when(now & (behind < FAR - 1))
            def _():
                to_left(k, behind).wait_recv()
                zsum[k] += zr[behind].astype(F32)

            @pl.when(now & (ahead >= 1) & (ahead <= FAR))
            def _():
                zout[k] = zsum[k].astype(BF16)
                to_right(k, ahead - 1).start()

            @pl.when(now & (ahead > FAR))
            def _():
                zout[k] = zsum[k].astype(BF16)
                to_left(k, behind - 1).start()

            @pl.when(now & (ahead == 0) & alone)
            def _():
                to_self(k).start()

            @pl.when(now & (ahead == 0) & jnp.logical_not(alone))
            def _():
                to_partner(k).start()

    def returns():
        out = []
        for k in range(1, SRC):
            to = lax.rem(dp + k, SRC)
            out.append(send(ret.at[to], got_ref.at[dp], rs.at[k], rr.at[k], others[k - 1]))
        return out

    keep = pltpu.make_async_copy(ret.at[dp], got_ref.at[dp], keep_sem)

    def one_expert(i, _):
        @pl.when(i < OWN)
        def _():
            @pl.when(i + 1 < OWN)
            def _():
                weight_copy(i + 1).start()

            weight_copy(i).wait()
            with jax.named_scope("expert"):
                expert_step(i, expert_at(i), wbuf, lax.rem(i, 2), gx, gh, gg, part, ret, late)
        @pl.when(jnp.logical_and(i >= 1, i <= OWN))
        def _():
            with jax.named_scope("combine"):
                combine(i - 1)

        @pl.when(i < OWN)
        def _():
            for one in first_sends(i):
                one.start()

        @pl.when(i == OWN - 1)
        def _():
            to = lax.broadcasted_iota(jnp.int32, (OWN * MAIN, OWN * MAIN), 0)
            source = lax.broadcasted_iota(jnp.int32, (OWN * MAIN, OWN * MAIN), 1)
            want = (lax.rem(to, 16) // 2) * 16 + (to // 16) * 2 + lax.rem(to, 2)
            shuffle = (source == want).astype(F32).astype(BF16)
            moved = jnp.dot(shuffle, late[...], preferred_element_type=F32).astype(BF16)
            ret[:, OWN * MAIN :, :] = moved.reshape(SRC, OWN * OVER, 2 * HD)
            for one in returns():
                one.start()
            keep.start()

        @pl.when(jnp.logical_and(i >= 2, i <= OWN + 1))
        def _():
            with jax.named_scope("finish"):
                finish(i - 2)
            with jax.named_scope("along"):
                along(i - 2, False)

        @pl.when(i >= 3)
        def _():
            with jax.named_scope("lagging"):
                along(i - 3, True)

        return 0

    lax.fori_loop(0, OWN + 3, one_expert, 0)
    with jax.named_scope("returned"):
        for one in returns():
            one.wait()
        keep.wait()

    @pl.when(jnp.logical_not(alone))
    def _():
        to_partner(0).wait_recv()

    def drain(i, _):
        for one in first_sends(i) + second_sends(i):
            one.wait_send()
        for c in range(2):
            k = 2 * i + c
            last = (i == OWN - 1) & (lax.rem(z, 2) == c)

            @pl.when(jnp.logical_not(last))
            def _():
                to_right(k, 0).wait_send()

            @pl.when(last & alone)
            def _():
                to_self(k).wait()

            @pl.when(last & jnp.logical_not(alone))
            def _():
                to_partner(k).wait_send()

        return 0

    lax.fori_loop(0, OWN, drain, 0)
    for n in range(8):
        for one in tokens(n):
            one.wait_send()
    for hop in range(FAR):
        for way in range(2):
            if hop < FAR - way:
                along_z(mine_z, z, way, hop).wait_send()
                bundle(z, way, hop).wait_send()
    for way in range(2):
        early_y(way).wait_send()
        early_forward(y2, way).wait_send()

    def drain_y(col, _):
        for way in range(2):
            along_y(mine_z, col, way).wait_send()
            forward(y2, col, way).wait_send()
        return 0

    lax.fori_loop(0, 16, drain_y, 0)


def owner_work(grads, small, proj):
    sems = pltpu.SemaphoreType.DMA
    vmem = pltpu.VMEM
    return pl.pallas_call(
        owner_kernel,
        out_shape=(
            jax.ShapeDtypeStruct((16, D), F32),
            jax.ShapeDtypeStruct((SRC, ROWS, 2 * HD), BF16),
            jax.ShapeDtypeStruct((4, 16, 16, D), BF16),
        ),
        in_specs=[pl.BlockSpec(memory_space=pl.ANY)] * 3,
        out_specs=(pl.BlockSpec(memory_space=pl.ANY),) * 3,
        scratch_shapes=[
            vmem((SRC, TOK, D), BF16),
            vmem((SRC, TOK, TOPK * HD + 128), BF16),
            vmem((16, D), BF16),
            vmem((2, 4, 2, 16, D), BF16),
            vmem((OWN, ROWS, D), BF16),
            vmem((OWN, ROWS, HD), BF16),
            vmem((OWN, ROWS, 128), F32),
            vmem((TOPK * TOK, 2 * HD), BF16),
            vmem((OWN * MAIN, TOPK * TOK), BF16),
            vmem((OWN * MAIN, TOPK * TOK), BF16),
            vmem((OWN * MAIN, SRC * TOK), BF16),
            vmem((OWN * MAIN, 2 * HD), F32),
            vmem((OWN, 4, 32, D), BF16),
            vmem((OWN, 2, 32, HALF), BF16),
            vmem((OWN, 2, 32, D), BF16),
            vmem((OWN, 2, 32, HALF), BF16),
            vmem((FAR, 16, D), BF16),
            vmem((FAR - 1, 16, D), BF16),
            vmem((2 * OWN, 16, D), BF16),
            vmem((2 * OWN, 16, D), F32),
            vmem((SRC, ROWS, 2 * HD), BF16),
            vmem((OWN * MAIN, 2 * HD), BF16),
            sems((2,)),
            sems((8, 2)),
            sems((8, 2)),
            sems((2,)),
            sems,
            sems((2, FAR)),
            sems((2, FAR)),
            sems((2, 16)),
            sems((2, 16)),
            sems((2, 16)),
            sems((2, 16)),
            sems((4,)),
            sems((4,)),
            sems((2, FAR)),
            sems((2, FAR)),
            sems((2,)),
            sems((OWN, 4)),
            sems((OWN, 4)),
            sems((OWN, 2)),
            sems((OWN, 2)),
            sems((2 * OWN,)),
            sems((FAR,)),
            sems((FAR - 1,)),
            sems,
            sems((SRC,)),
            sems((SRC,)),
            sems,
        ],
        compiler_params=pltpu.CompilerParams(
            collective_id=0, has_side_effects=True, vmem_limit_bytes=67043328
        ),
    )(grads, small, proj)


def return_kernel(routes_ref, back_ref, head_ref, gate_ref):
    routes = routes_ref[...]
    experts = lax.broadcasted_iota(jnp.int32, (TOK, 128), 1)
    named = [(routes[:, k : k + 1] == experts).astype(F32) for k in range(TOPK)]
    chosen = functools.reduce(lambda a, b: a + b, named)
    lower = (iota((TOK, TOK), 1) < iota((TOK, TOK), 0)).astype(BF16)
    before = jnp.dot(lower, chosen.astype(BF16), preferred_element_type=F32)
    rows = lax.broadcasted_iota(jnp.int32, (TOK, SRC * ROWS), 1)
    gates = jnp.zeros((TOK, 128), F32)
    for k in range(TOPK):
        expert = routes[:, k : k + 1]
        slot = jnp.sum(named[k] * before, axis=1, keepdims=True).astype(jnp.int32)
        owner = 2 * (expert >> 4) + (expert & 1)
        index = (expert & 15) >> 1
        place = jnp.where(
            slot < MAIN, index * MAIN + slot, OWN * MAIN + OVER * index + slot - MAIN
        )
        pick = (rows == owner * ROWS + place).astype(F32).astype(BF16)
        block = jnp.dot(pick, back_ref[...], preferred_element_type=F32)
        head_ref[:, k * HD : (k + 1) * HD] = block[:, 0:HD].astype(BF16)
        gates = jnp.where(experts == k, block[:, HD:], gates)
    gate_ref[...] = gates[:, 0:TOPK].astype(BF16)


def put_back(routes, back):
    return pl.pallas_call(
        return_kernel,
        out_shape=(
            jax.ShapeDtypeStruct((TOK, TOPK * HD), BF16),
            jax.ShapeDtypeStruct((TOK, TOPK), BF16),
        ),
        compiler_params=pltpu.CompilerParams(vmem_limit_bytes=32 << 20),
    )(routes, back)


def local(head_outputs, out_grad, gate_weights, route_ids, out_proj):
    small = jnp.concatenate(
        [
            head_outputs.reshape(TOK, TOPK * HD),
            gate_weights,
            route_ids.astype(BF16),
            jnp.zeros((TOK, 128 - 2 * TOPK), BF16),
        ],
        axis=1,
    )
    grad_proj, got, _ = owner_work(out_grad, small, out_proj[0])
    grad_head, grad_gate = put_back(route_ids, got.reshape(SRC * ROWS, 2 * HD))
    return grad_head.reshape(TOK, TOPK, HD), grad_gate, grad_proj[None]


def solution(mesh):
    return jax.shard_map(
        local,
        mesh=mesh,
        in_specs=(
            P(("dp", "expert"), None, None),
            P(("dp", "expert"), None),
            P(("dp", "expert"), None),
            P(("dp", "expert"), None),
            P("expert", None, None),
        ),
        out_specs=(
            P(("dp", "expert"), None, None),
            P(("dp", "expert"), None),
            P("expert", "dp", None),
        ),
        check_vma=False,
    )
```
